32 devices in a mesh: groups: 2 (over y), ctx: 4 (over z), head: 2 (over x), sub: 2 (over core).
Axes of the slice: x: 2, y: 2, z: 4, core: 2. Of those that a mesh axis runs over, the one named last changes fastest.
Arguments:
- tokens: bfloat16 [16384, 3584], P(('groups', 'ctx', 'sub'), 'head'), parts along dimension 0, may hold values from -40 to 40
- q_weight: bfloat16 [3584, 3584], P('sub', 'head'), may hold values from -0.09375 to 0.09375
- k_weight: bfloat16 [3584, 512], P('sub', 'head'), may hold values from -0.09375 to 0.09375
- v_weight: bfloat16 [3584, 512], P('sub', 'head'), may hold values from -0.09375 to 0.09375
- q_bias: float32 [3584], P('head'), may hold values from -3 to 3
- v_bias: float32 [512], P('head'), may hold values from -3 to 3
Outputs:
- head_outputs: bfloat16 [16384, 3584], P(('groups', 'ctx', 'sub')), parts along dimension 0
The draws below stay inside these ranges and needn't reach their ends.
There are 2 independent parts, one for each index of `groups`. The reference program is written for one: setup_inputs(seed, part) draws one part's arguments, and reference() takes and returns one part's arrays. A program takes and returns all parts, laid end to end along the dimension named above; an argument that names none is the same for every part. Nothing has to cross between parts.
All inputs are finite; a program needn't handle non-finite values.
Results may differ from the reference program's by a relative error of at most 0.0059.
Values may be sent and summed in bfloat16 or wider, within the bound.
No kernel may reach another device: no remote copies, remote signals or barrier semaphores. Data moves between devices by JAX's collectives and lax.ppermute only.
A program may use at most 128 MiB of HBM per device.

```python
import math
import jax
import jax.numpy as jnp
from jax import lax

D = 3584
HQ = 28
KVH = 4
HD = 128
BLOCK = 128
BLK_DEV = 8
WINDOW = 8192


def draw_tokens(key, part):
    first_key = jax.random.fold_in(jax.random.fold_in(key, 17), 0)
    noise = jax.random.normal(first_key, (WINDOW, D), jnp.float32)
    values = noise
    return jnp.clip(values, -40.0, 40.0).astype(jnp.bfloat16)


def steps_of(own_key, dims, cuts, smallest, top_value):
    factor_of = 1.0
    for position, parts in cuts:
        heights = jax.random.uniform(jax.random.fold_in(jax.random.fold_in(own_key, 6), position), (parts,), jnp.float32, smallest / len(cuts), top_value / len(cuts))
        factor_of = factor_of * jnp.repeat(jnp.exp(heights), dims[position] // parts).reshape((-1,) + (1,) * (len(dims) - 1 - position))
    return factor_of


def scatter_about(stream_key, shape, spread, reach, cuts=(), kind=jnp.bfloat16):
    drawn = spread * jax.random.normal(stream_key, shape, jnp.float32)
    if cuts:
        drawn = drawn * steps_of(stream_key, shape, cuts, -0.22, 0.18)
    return jnp.clip(drawn, -reach, reach).astype(kind)


def setup_inputs(seed: int = 0, part: int = 0) -> dict:
    seeds = jax.random.split(jax.random.key(seed), 7)
    own_keys = jax.random.split(jax.random.fold_in(seeds[6], part), 7)
    tokens = draw_tokens(jax.random.fold_in(jax.random.fold_in(seeds[6], part), 71), part)
    q_weight = scatter_about(seeds[1], (D, HQ * HD), D ** -0.5, 0.09375, ((0, 2), (1, 2)))
    k_weight = scatter_about(seeds[2], (D, KVH * HD), D ** -0.5, 0.09375, ((0, 2), (1, 2)))
    v_weight = scatter_about(seeds[3], (D, KVH * HD), D ** -0.5, 0.09375, ((0, 2), (1, 2)))
    q_bias = scatter_about(seeds[4], (HQ * HD,), 0.5, 3.0, ((0, 2),), jnp.float32)
    v_bias = scatter_about(seeds[5], (KVH * HD,), 0.5, 3.0, ((0, 2),), jnp.float32)
    return {"tokens": tokens, "q_weight": q_weight, "k_weight": k_weight, "v_weight": v_weight, "q_bias": q_bias, "v_bias": v_bias}


def rotate(values, positions):
    half = values.shape[-1] // 2
    freqs = jnp.exp(-(2.0 * jnp.arange(half, dtype=jnp.float32) / (2 * half)) * math.log(1000000.0))
    angle = positions[:, None] * freqs[None, :]
    cosine = jnp.cos(angle)[:, None, :]
    sine = jnp.sin(angle)[:, None, :]
    first = values[..., :half]
    second = values[..., half:]
    return jnp.concatenate([first * cosine - second * sine, second * cosine + first * sine], axis=-1)

def reference(tokens, q_weight, k_weight, v_weight, q_bias, v_bias):
    group = HQ // KVH
    nblocks = WINDOW // BLOCK
    positions = jnp.arange(WINDOW, dtype=jnp.float32)
    distances = jnp.array([0, 1, 2, 4, 8, 16, 32, 64, 128], dtype=jnp.int32)
    scale = 1.0 / math.sqrt(HD)
    lower = jnp.arange(BLOCK, dtype=jnp.int32)[:, None] >= jnp.arange(BLOCK, dtype=jnp.int32)[None, :]
    notself = jnp.arange(9, dtype=jnp.int32) != 0

    def one_head(head_index):
        w_query = lax.dynamic_slice_in_dim(q_weight, head_index * group * HD, group * HD, 1)
        w_key = lax.dynamic_slice_in_dim(k_weight, head_index * HD, HD, 1)
        w_value = lax.dynamic_slice_in_dim(v_weight, head_index * HD, HD, 1)
        query = jnp.dot(tokens, w_query, preferred_element_type=jnp.float32) + lax.dynamic_slice_in_dim(q_bias, head_index * group * HD, group * HD, 0)
        keyed = jnp.dot(tokens, w_key, preferred_element_type=jnp.float32)
        valued = jnp.dot(tokens, w_value, preferred_element_type=jnp.float32) + lax.dynamic_slice_in_dim(v_bias, head_index * HD, HD, 0)
        query = rotate(query.reshape(WINDOW, group, HD), positions).astype(jnp.bfloat16)
        keyed = rotate(keyed.reshape(WINDOW, 1, HD), positions).astype(jnp.bfloat16)
        valued = valued.astype(jnp.bfloat16)
        key_blocks = keyed.reshape(nblocks, BLOCK, HD)
        value_blocks = valued.reshape(nblocks, BLOCK, HD)
        query_blocks = query.reshape(nblocks, BLOCK, group, HD)

        def one_group(start):
            global_block = start + jnp.arange(BLK_DEV, dtype=jnp.int32)
            query_group = lax.dynamic_slice_in_dim(query_blocks, start, BLK_DEV, 0)
            index = global_block[:, None] - distances[None, :]
            valid = index >= 0
            clipped = jnp.maximum(index, 0).astype(jnp.int32)
            keys = key_blocks[clipped].reshape(BLK_DEV, 9 * BLOCK, HD)
            vals = value_blocks[clipped].reshape(BLK_DEV, 9 * BLOCK, HD)
            mask = valid[:, None, :, None] & (notself[None, None, :, None] | lower[None, :, None, :])
            mask = mask.reshape(BLK_DEV, BLOCK, 9 * BLOCK)
            scores = jnp.einsum('bqgd,bsd->bgqs', query_group.astype(jnp.float32), keys.astype(jnp.float32)) * scale
            scores = jnp.where(mask[:, None], scores, -1e+30)
            peak = lax.optimization_barrier(jnp.max(scores, axis=-1, keepdims=True))
            expo = jnp.exp(scores - peak)
            weights = (expo / lax.optimization_barrier(jnp.sum(expo, axis=-1, keepdims=True))).astype(jnp.bfloat16)
            return jnp.einsum('bgqs,bsd->bqgd', weights.astype(jnp.float32), vals.astype(jnp.float32)).astype(jnp.bfloat16)
        starts = jnp.arange(0, nblocks, BLK_DEV, dtype=jnp.int32)
        result = lax.map(one_group, starts)
        return result.reshape(WINDOW, group * HD)
    every = lax.map(one_head, jnp.arange(KVH, dtype=jnp.int32))
    return jnp.transpose(every, (1, 0, 2)).reshape(WINDOW, HQ * HD)
```

```python
import functools
import math

import jax
import jax.numpy as jnp
from jax import lax
from jax.experimental import pallas as pl
from jax.experimental.pallas import tpu as pltpu
from jax.sharding import PartitionSpec as P

HQ = 28
KVH = 4
HD = 128
BLOCK = 128
NEAR = (0, 1, 2, 4)
GROUP = HQ // KVH
VMEM_LIMIT = 60 * 1024 * 1024


def shifted(value, axis, steps):
    count = lax.axis_size(axis)
    return lax.ppermute(value, axis, [(s, s + steps) for s in range(count - steps)])


def swapped(value, axis):
    return lax.ppermute(value, axis, [(0, 1), (1, 0)])


def rotary_tables(positions):
    half = HD // 2
    freqs = jnp.exp(-(2.0 * jnp.arange(half, dtype=jnp.float32) / (2 * half)) * math.log(1000000.0))
    angle = positions[:, None] * freqs[None, :]
    cosine = jnp.cos(angle)
    sine = jnp.sin(angle)
    return jnp.concatenate([cosine, cosine], 1), jnp.concatenate([-sine, sine], 1)


def project_body(kvl, flag, ta, tb, wqa, wqb, wka, wkb, wva, wvb, qb, vb, cos, sin, q_out, kv_out, xs):
    step = pl.program_id(0)
    half = ta.shape[1]

    @pl.when(step == 0)
    def _():
        @pl.when(flag[0] == 1)
        def _():
            xs[:, :half] = ta[...]
            xs[:, half:] = tb[...]

        @pl.when(flag[0] != 1)
        def _():
            xs[:, :half] = tb[...]
            xs[:, half:] = ta[...]

    def mm(wa, wb):
        return jnp.dot(xs[:, :half], wa[...], preferred_element_type=jnp.float32) + jnp.dot(
            xs[:, half:], wb[...], preferred_element_type=jnp.float32
        )

    def rope(v):
        return v * cos[...] + pltpu.roll(v, HD // 2, 1) * sin[...]

    @pl.when(step == 0)
    def _():
        k = mm(wka, wkb)
        v = mm(wva, wvb) + vb[...]
        for h in range(kvl):
            kv_out[:, h * HD : (h + 1) * HD] = rope(k[:, h * HD : (h + 1) * HD]).astype(jnp.bfloat16)
        kv_out[:, kvl * HD :] = v.astype(jnp.bfloat16)

    acc = mm(wqa, wqb) + qb[...]
    for h in range(acc.shape[1] // HD):
        q_out[:, h * HD : (h + 1) * HD] = rope(acc[:, h * HD : (h + 1) * HD]).astype(jnp.bfloat16)


def project(flag, ta, ta_row, tb, tb_row, rows, weights, qb, vb, cos, sin, cs_row):
    wqa, wqb, wka, wkb, wva, wvb = weights
    half, nq = wqa.shape
    nk = wka.shape[1]
    tile = 2 * HD if nq % (2 * HD) == 0 else HD
    grid = (nq // tile,)
    whole = lambda r, c, at=0: pl.BlockSpec((r, c), lambda i, f: (at, 0))
    col = lambda r: pl.BlockSpec((r, tile), lambda i, f: (0, i))
    flops = 2 * rows * 2 * half * (nq + 2 * nk)
    return pl.pallas_call(
        functools.partial(project_body, nk // HD),
        out_shape=(
            jax.ShapeDtypeStruct((rows, nq), jnp.bfloat16),
            jax.ShapeDtypeStruct((rows, 2 * nk), jnp.bfloat16),
        ),
        grid_spec=pltpu.PrefetchScalarGridSpec(
            num_scalar_prefetch=1,
            grid=grid,
            in_specs=[
                whole(rows, half, ta_row), whole(rows, half, tb_row),
                col(half), col(half),
                whole(half, nk), whole(half, nk), whole(half, nk), whole(half, nk),
                col(1), whole(1, nk),
                whole(rows, HD, cs_row), whole(rows, HD, cs_row),
            ],
            out_specs=[pl.BlockSpec((rows, tile), lambda i, f: (0, i)), whole(rows, 2 * nk)],
            scratch_shapes=[pltpu.VMEM((rows, 2 * half), jnp.bfloat16)],
        ),
        compiler_params=pltpu.CompilerParams(vmem_limit_bytes=VMEM_LIMIT),
        cost_estimate=pl.CostEstimate(
            flops=flops, bytes_accessed=2 * (2 * half * (nq + 2 * nk) + rows * 2 * half), transcendentals=0
        ),
        name="project",
    )(flag, ta, tb, wqa, wqb, wka, wkb, wva, wvb, qb, vb, cos, sin)


def attend_body(plan, n_arrays, bias, *refs):
    nb = len(plan)
    q_refs = refs[:nb]
    k_refs = refs[nb : nb + n_arrays]
    v_refs = refs[nb + n_arrays : nb + 2 * n_arrays]
    out = refs[nb + 2 * n_arrays]
    scale = math.log2(math.e) / math.sqrt(HD)
    for j, slots in enumerate(plan):
        n = len(slots)
        block = lambda rs, a, r: rs[a][r * BLOCK : (r + 1) * BLOCK, :]
        keys = jnp.concatenate([block(k_refs, a, r) for a, r in slots], 0)
        vals = jnp.concatenate([block(v_refs, a, r) for a, r in slots], 0)
        vals = jnp.concatenate([vals, jnp.ones_like(vals)], 1)
        query = q_refs[j]
        lower = lax.broadcasted_iota(jnp.int32, (BLOCK, BLOCK), 0) >= lax.broadcasted_iota(
            jnp.int32, (BLOCK, BLOCK), 1
        )
        for h in range(GROUP):
            s = lax.dot_general(
                query[:, h * HD : (h + 1) * HD], keys, (((1,), (1,)), ((), ())),
                preferred_element_type=jnp.float32,
            )
            parts = [jnp.where(lower, s[:, :BLOCK], -1e30)]
            for t in range(1, n):
                parts.append(s[:, t * BLOCK : (t + 1) * BLOCK] + bias[j * n + t])
            s = jnp.concatenate(parts, 1)
            peak = jnp.max(s, axis=1, keepdims=True)
            p = jnp.exp2((s - peak) * scale).astype(jnp.bfloat16)
            o = jnp.dot(p, vals, preferred_element_type=jnp.float32)
            out[j * BLOCK : (j + 1) * BLOCK, h * HD : (h + 1) * HD] = (o[:, :HD] / o[:, HD:]).astype(jnp.bfloat16)


def attend(bias, queries, arrays, plan, kvl):
    nb = len(queries)
    width = GROUP * HD
    q_specs = [pl.BlockSpec((BLOCK, width), lambda g, f, at=r: (at, g)) for _, r in queries]
    k_specs = [pl.BlockSpec((a.shape[0], HD), lambda g, f: (0, g)) for a in arrays]
    v_specs = [pl.BlockSpec((a.shape[0], HD), lambda g, f: (0, kvl + g)) for a in arrays]
    keys = len(plan[0]) * BLOCK
    return pl.pallas_call(
        functools.partial(attend_body, plan, len(arrays)),
        out_shape=jax.ShapeDtypeStruct((nb * BLOCK, kvl * width), jnp.bfloat16),
        grid_spec=pltpu.PrefetchScalarGridSpec(
            num_scalar_prefetch=1,
            grid=(kvl,),
            in_specs=q_specs + k_specs + v_specs,
            out_specs=pl.BlockSpec((nb * BLOCK, width), lambda g, f: (0, g)),
        ),
        compiler_params=pltpu.CompilerParams(vmem_limit_bytes=VMEM_LIMIT),
        cost_estimate=pl.CostEstimate(
            flops=8 * nb * kvl * width * keys * BLOCK,
            bytes_accessed=4 * nb * BLOCK * kvl * width,
            transcendentals=nb * BLOCK * kvl * GROUP * keys,
        ),
        name="attend",
    )(bias, *[a for a, _ in queries], *arrays, *arrays)


def place_body(side, src, *rest):
    rest[-1][...] = src[...]


def place(total, piece, side, blocks, shape):
    nb = len(blocks)
    cols = piece.shape[1]
    step = blocks[1] - blocks[0] if nb > 1 else 0
    in_specs = [pl.BlockSpec((BLOCK, cols), lambda i, s: (i, 0))]
    args = [piece]
    aliases = {}
    if total is not None:
        in_specs.append(pl.BlockSpec(memory_space=pl.ANY))
        args.append(total)
        aliases = {2: 0}
    return pl.pallas_call(
        place_body,
        out_shape=jax.ShapeDtypeStruct(shape, jnp.bfloat16),
        grid_spec=pltpu.PrefetchScalarGridSpec(
            num_scalar_prefetch=1,
            grid=(nb,),
            in_specs=in_specs,
            out_specs=pl.BlockSpec((BLOCK, cols), lambda i, s: (blocks[0] + i * step, s[0])),
        ),
        input_output_aliases=aliases,
        cost_estimate=pl.CostEstimate(flops=0, bytes_accessed=4 * nb * BLOCK * cols, transcendentals=0),
        name="place",
    )(side, *args)


def chunks_of(blocks):
    runs = [(b, min(2, blocks - 2 - b)) for b in range(0, blocks - 2, 2)]
    return runs + [(blocks - 2, 1), (blocks - 1, 1)]


def order_of(blocks):
    late = lambda b: max([blocks + b - d for d in NEAR if d > b] + [b])
    ranked = sorted(range(blocks), key=lambda b: (max(late(b), 0), -b))
    return [tuple(ranked[i : i + 2]) for i in range(0, blocks, 2)]


def on_device(tokens, q_weight, k_weight, v_weight, q_bias, v_bias):
    n_sub = lax.axis_size("sub")
    n_ctx = lax.axis_size("ctx")
    n_head = lax.axis_size("head")
    rows = tokens.shape[0]
    blocks = rows // BLOCK
    kvl = k_weight.shape[1] // HD
    sub = lax.axis_index("sub")
    ctx = lax.axis_index("ctx")
    head = lax.axis_index("head")
    shard = ctx * n_sub + sub
    runs = chunks_of(blocks)

    paired = n_head == 2
    if paired:
        pieces = [swapped(tokens[b * BLOCK : (b + n) * BLOCK], "head") for b, n in runs]
        flag = (sub == head).astype(jnp.int32).reshape(1)
    else:
        features = lax.all_gather(tokens, "head", axis=1, tiled=True)
        half = features.shape[1] // n_sub
        flag = (sub == 0).astype(jnp.int32).reshape(1)
        tokens = features[:, :half]
        pieces = [features[b * BLOCK : (b + n) * BLOCK, half:] for b, n in runs]
    weights = (
        q_weight, swapped(q_weight, "sub"),
        k_weight, swapped(k_weight, "sub"),
        v_weight, swapped(v_weight, "sub"),
    )
    qb = q_bias[None, :]
    vb = v_bias[None, :]
    positions = (shard * rows + jnp.arange(rows, dtype=jnp.int32)).astype(jnp.float32)
    cos, sin = rotary_tables(positions)

    far_steps = [s for s in (1, 2, 4, 8) if s < n_ctx]
    queries, sources = {}, {}
    for (b, n), piece in zip(runs, pieces):
        q, kv = project(flag, tokens, b // n, piece, 0, n * BLOCK, weights, qb, vb, cos, sin, b // n)
        far = {}
        for s in far_steps:
            far[s] = shifted(kv, "ctx", 1) if s == 1 else shifted(far[s // 2], "ctx", s // 2)
        held = {"own": kv, "prev": shifted(kv, ("ctx", "sub"), 1)}
        held.update({("far", s): far[s] for s in far_steps})
        for r in range(n):
            queries[b + r] = (q, r)
            for name, array in held.items():
                sources[name, b + r] = (array, r)

    shape = (rows, n_head * q_weight.shape[1])
    mine = head.astype(jnp.int32).reshape(1)
    total = None
    outs = {}
    results = []
    for pair in order_of(blocks):
        arrays, plan, distances = [], [], []
        for b in pair:
            slots = []
            wanted = [(d, ("own", b - d) if d <= b else ("prev", blocks + b - d)) for d in NEAR + (blocks,)]
            wanted += [(n_sub * blocks * s, (("far", s), b)) for s in far_steps]
            for d, key in wanted:
                array, r = sources[key]
                at = next((i for i, a in enumerate(arrays) if a is array), None)
                if at is None:
                    at = len(arrays)
                    arrays.append(array)
                slots.append((at, r))
                distances.append(b - d)
            plan.append(tuple(slots))
        valid = shard * blocks + jnp.array(distances, jnp.int32) >= 0
        bias = jnp.where(valid, 0.0, -1e30).astype(jnp.float32)
        own = attend(bias, [queries[b] for b in pair], arrays, plan, kvl)
        if paired:
            results.append((pair, own, swapped(own, "head")))
        else:
            for i, b in enumerate(pair):
                outs[b] = own[i * BLOCK : (i + 1) * BLOCK]
    if not paired:
        local = jnp.concatenate([outs[b] for b in range(blocks)], 0)
        return lax.all_gather(local, "head", axis=1, tiled=True)
    for pair, own, _ in results:
        total = place(total, own, mine, pair, shape)
    for pair, _, other in results:
        total = place(total, other, 1 - mine, pair, shape)
    return total


def solution(mesh):
    return jax.shard_map(
        on_device,
        mesh=mesh,
        in_specs=(
            P(("groups", "ctx", "sub"), "head"),
            P("sub", "head"),
            P("sub", "head"),
            P("sub", "head"),
            P("head"),
            P("head"),
        ),
        out_specs=P(("groups", "ctx", "sub"), None),
        check_vma=False,
    )
```

```python
import functools
import math

import jax
import jax.numpy as jnp
from jax import lax
from jax.experimental import pallas as pl
from jax.experimental.pallas import tpu as pltpu
from jax.sharding import PartitionSpec as P


HQ = 28
KVH = 4
HD = 128
BLOCK = 128
NEAR = (0, 1, 2, 4)
GROUP = HQ // KVH


def shifted(value, axis, steps):
    count = lax.axis_size(axis)
    return lax.ppermute(value, axis, [(s, (s + steps) % count) for s in range(count)])


def swapped(value, axis):
    return lax.ppermute(value, axis, [(0, 1), (1, 0)])


def rotary_tables(positions):
    half = HD // 2
    freqs = jnp.exp(-(2.0 * jnp.arange(half, dtype=jnp.float32) / (2 * half)) * math.log(1000000.0))
    angle = positions[:, None] * freqs[None, :]
    cosine = jnp.cos(angle)
    sine = jnp.sin(angle)
    return jnp.concatenate([cosine, cosine], 1), jnp.concatenate([-sine, sine], 1)


VMEM = pl.BlockSpec(memory_space=pltpu.VMEM)
SMEM = pl.BlockSpec(memory_space=pltpu.SMEM)
ANY = pl.BlockSpec(memory_space=pl.ANY)
HBM = pl.BlockSpec(memory_space=pltpu.HBM)


def params(mib):
    return pltpu.CompilerParams(vmem_limit_bytes=mib * 2**20)


def stage_body(n, flag, *refs):
    own, other, outs, sems = refs[:n], refs[n : 2 * n], refs[2 * n : -1], refs[-1]

    def bring(first, second):
        copies = []
        for half, sources in enumerate((first, second)):
            q_out, kv_out = outs[2 * half], outs[2 * half + 1]
            nk = sources[1].shape[1]
            targets = (q_out, kv_out.at[:, pl.ds(0, nk)], kv_out.at[:, pl.ds(nk, nk)])
            for i, (source, target) in enumerate(zip(sources, targets)):
                copies.append(pltpu.make_async_copy(source, target, sems.at[half, i]))
        for copy in copies:
            copy.start()
        for copy in copies:
            copy.wait()

    @pl.when(flag[0] == 1)
    def _():
        bring(own, other)

    @pl.when(flag[0] != 1)
    def _():
        bring(other, own)


def stage(flag, own, other):
    half, nq = own[0].shape
    nk = own[1].shape[1]
    shapes = [pltpu.VMEM((half, nq), jnp.bfloat16), pltpu.VMEM((half, 2 * nk), jnp.bfloat16)] * 2
    return pl.pallas_call(
        functools.partial(stage_body, len(own)),
        out_shape=tuple(shapes),
        in_specs=[SMEM] + [HBM] * (2 * len(own)),
        out_specs=(VMEM,) * 4,
        scratch_shapes=[pltpu.SemaphoreType.DMA((2, len(own)))],
        compiler_params=params(2),
        cost_estimate=pl.CostEstimate(flops=0, bytes_accessed=4 * half * (nq + 2 * nk), transcendentals=0),
        name="stage",
    )(flag, *own, *other)


def project_body(row, tile, rot, ta, tb, wa, wb, bias, cos, sin, *refs):
    out = refs[-1]
    rows = tb.shape[0]
    mine = pl.ds(row, rows)

    def columns(i):
        at = pl.ds(pl.multiple_of(i * tile, tile), tile)
        acc = jnp.dot(ta[mine, :], wa[:, at], preferred_element_type=jnp.float32)
        acc = acc + jnp.dot(tb[...], wb[:, at], preferred_element_type=jnp.float32)
        acc = acc + bias[:, at]
        heads = []
        for h in range(tile // HD):
            v = acc[:, h * HD : (h + 1) * HD]
            if h < rot:
                v = v * cos[mine, :] + pltpu.roll(v, HD // 2, 1) * sin[mine, :]
            heads.append(v.astype(jnp.bfloat16))
        out[:, at] = jnp.concatenate(heads, 1)

    if tile == out.shape[1]:
        columns(0)
    else:
        pl.loop(0, out.shape[1] // tile)(columns)


def project(tokens, row, piece, wa, wb, bias, cos, sin, tile, rot, deps):
    rows, half = piece.shape
    cols = wa.shape[1]
    return pl.pallas_call(
        functools.partial(project_body, row, tile, rot),
        out_shape=jax.ShapeDtypeStruct((rows, cols), jnp.bfloat16),
        in_specs=[VMEM] * 7 + [ANY] * len(deps),
        out_specs=VMEM,
        compiler_params=params(8),
        cost_estimate=pl.CostEstimate(flops=4 * rows * half * cols, bytes_accessed=0, transcendentals=0),
    )(tokens, piece, wa, wb, bias, cos, sin, *deps)


def attend_body(plan, n_arrays, kvl, bias, *refs):
    nb = len(plan)
    arrays = refs[nb : nb + n_arrays]
    out = refs[-1]
    scale = math.log2(math.e) / math.sqrt(HD)
    lower = lax.broadcasted_iota(jnp.int32, (BLOCK, BLOCK), 0) >= lax.broadcasted_iota(
        jnp.int32, (BLOCK, BLOCK), 1
    )

    def kv_head(g):
        for j, (q_row, slots) in enumerate(plan):
            n = len(slots)
            k_at = pl.ds(pl.multiple_of(g * HD, HD), HD)
            v_at = pl.ds(pl.multiple_of((kvl + g) * HD, HD), HD)
            keys = jnp.concatenate([arrays[a][r * BLOCK : (r + 1) * BLOCK, k_at] for a, r in slots], 0)
            vals = jnp.concatenate([arrays[a][r * BLOCK : (r + 1) * BLOCK, v_at] for a, r in slots], 0)
            vals = jnp.concatenate([vals, jnp.ones_like(vals)], 1)
            for h in range(GROUP):
                at = pl.ds(pl.multiple_of((g * GROUP + h) * HD, HD), HD)
                s = lax.dot_general(
                    refs[j][q_row * BLOCK : (q_row + 1) * BLOCK, at], keys, (((1,), (1,)), ((), ())),
                    preferred_element_type=jnp.float32,
                )
                parts = [jnp.where(lower, s[:, :BLOCK], -1e30)]
                for t in range(1, n):
                    parts.append(s[:, t * BLOCK : (t + 1) * BLOCK] + bias[j * n + t])
                s = jnp.concatenate(parts, 1)
                peak = jnp.max(s, axis=1, keepdims=True)
                p = jnp.exp2((s - peak) * scale).astype(jnp.bfloat16)
                o = jnp.dot(p, vals, preferred_element_type=jnp.float32)
                out[j * BLOCK : (j + 1) * BLOCK, at] = (o[:, :HD] / o[:, HD:]).astype(jnp.bfloat16)

    if kvl == 1:
        kv_head(0)
    else:
        pl.loop(0, kvl)(kv_head)


def attend(bias, queries, arrays, plan, kvl, deps):
    nb = len(queries)
    width = kvl * GROUP * HD
    keys = len(plan[0]) * BLOCK
    plan = [(r, slots) for (_, r), slots in zip(queries, plan)]
    return pl.pallas_call(
        functools.partial(attend_body, plan, len(arrays), kvl),
        out_shape=jax.ShapeDtypeStruct((nb * BLOCK, width), jnp.bfloat16),
        in_specs=[SMEM] + [VMEM] * (nb + len(arrays)) + [ANY] * len(deps),
        out_specs=VMEM,
        compiler_params=params(8),
        cost_estimate=pl.CostEstimate(
            flops=8 * nb * width * keys * BLOCK,
            bytes_accessed=0,
            transcendentals=nb * BLOCK * kvl * GROUP * keys,
        ),
        name="attend",
    )(bias, *[a for a, _ in queries], *arrays, *deps)


def cut_body(row, source, out, sem):
    copy = pltpu.make_async_copy(source.at[pl.ds(row, out.shape[0]), :], out, sem)
    copy.start()
    copy.wait()


def cut(source, block, count):
    return pl.pallas_call(
        functools.partial(cut_body, block * BLOCK),
        out_shape=pltpu.VMEM((count * BLOCK, source.shape[1]), source.dtype),
        in_specs=[HBM],
        out_specs=VMEM,
        scratch_shapes=[pltpu.SemaphoreType.DMA],
        compiler_params=params(2),
        cost_estimate=pl.CostEstimate(
            flops=0, bytes_accessed=2 * count * BLOCK * source.shape[1], transcendentals=0
        ),
        name="cut",
    )(source)


def place_body(side, src, *rest):
    rest[-1][...] = src[...]


def place(total, piece, side, blocks, shape):
    nb = len(blocks)
    cols = piece.shape[1]
    step = blocks[1] - blocks[0] if nb > 1 else 0
    in_specs = [pl.BlockSpec((BLOCK, cols), lambda i, s: (i, 0))]
    args = [piece]
    aliases = {}
    if total is not None:
        in_specs.append(pl.BlockSpec(memory_space=pl.ANY))
        args.append(total)
        aliases = {2: 0}
    return pl.pallas_call(
        place_body,
        out_shape=jax.ShapeDtypeStruct(shape, jnp.bfloat16),
        grid_spec=pltpu.PrefetchScalarGridSpec(
            num_scalar_prefetch=1,
            grid=(nb,),
            in_specs=in_specs,
            out_specs=pl.BlockSpec((BLOCK, cols), lambda i, s: (blocks[0] + i * step, s[0])),
        ),
        input_output_aliases=aliases,
        compiler_params=params(4),
        cost_estimate=pl.CostEstimate(flops=0, bytes_accessed=4 * nb * BLOCK * cols, transcendentals=0),
        name="place",
    )(side, *args)


def chunks_of(blocks):
    n = blocks // 4
    return [(quarter * n, n) for quarter in (2, 0, 1, 3)]


def layer(tokens, q_weight, k_weight, v_weight, q_bias, v_bias):
    n_sub = lax.axis_size("sub")
    n_ctx = lax.axis_size("ctx")
    n_head = lax.axis_size("head")
    rows = tokens.shape[0]
    blocks = rows // BLOCK
    kvl = k_weight.shape[1] // HD
    sub = lax.axis_index("sub")
    ctx = lax.axis_index("ctx")
    head = lax.axis_index("head")
    shard = ctx * n_sub + sub
    runs = chunks_of(blocks)

    paired = n_head == 2
    if paired:
        pieces = []
        for b, n in runs:
            pieces.append(swapped(cut(tokens, b, n), "head"))
        flag = (sub == head).astype(jnp.int32).reshape(1)
    else:
        features = lax.all_gather(tokens, "head", axis=1, tiled=True)
        half = features.shape[1] // n_sub
        flag = (sub == 0).astype(jnp.int32).reshape(1)
        tokens = features[:, :half]
        pieces = [features[b * BLOCK : (b + n) * BLOCK, half:] for b, n in runs]
    own = (q_weight, k_weight, v_weight)
    other = swapped(k_weight, "sub"), swapped(v_weight, "sub")
    other = (swapped(q_weight, "sub"),) + other
    wqa, wkva, wqb, wkvb = stage(flag, own, other)
    qb = q_bias[None, :]
    kvb = jnp.concatenate([jnp.zeros_like(v_bias), v_bias])[None, :]
    positions = (shard * rows + jnp.arange(rows, dtype=jnp.int32)).astype(jnp.float32)
    cos, sin = rotary_tables(positions)

    far_steps = [s for s in (1, 2, 4, 8) if s < n_ctx]
    queries, sources = {}, {}
    deps = ()

    def keys_values(i, deps):
        (b, n), piece = runs[i], pieces[i]
        kv = project(tokens, b * BLOCK, piece, wkva, wkvb, kvb, cos, sin, 2 * kvl * HD, kvl, deps)
        held = {"own": kv}
        held["prev"] = shifted(kv, ("ctx", "sub"), 1)
        for s in far_steps:
            held["far", s] = shifted(kv, "ctx", 1) if s == 1 else shifted(held["far", s // 2], "ctx", s // 2)
        for r in range(n):
            for name, array in held.items():
                sources[name, b + r] = (array, r)
        return (kv,)

    def all_queries(i, deps):
        (b, n), piece = runs[i], pieces[i]
        tile = 2 * HD if q_weight.shape[1] % (2 * HD) == 0 else HD
        q = project(tokens, b * BLOCK, piece, wqa, wqb, qb, cos, sin, tile, tile // HD, deps)
        for r in range(n):
            queries[b + r] = (q, r)
        return (q,)

    mine = head.astype(jnp.int32).reshape(1)
    outs, results = {}, []

    def attention(pair, deps):
        arrays, plan, distances = [], [], []
        for b in pair:
            slots = []
            wanted = [(d, ("own", b - d) if d <= b else ("prev", blocks + b - d)) for d in NEAR + (blocks,)]
            wanted += [(n_sub * blocks * s, (("far", s), b)) for s in far_steps]
            for d, key in wanted:
                array, r = sources[key]
                at = next((i for i, a in enumerate(arrays) if a is array), None)
                if at is None:
                    at = len(arrays)
                    arrays.append(array)
                slots.append((at, r))
                distances.append(b - d)
            plan.append(tuple(slots))
        valid = shard * blocks + jnp.array(distances, jnp.int32) >= 0
        bias = jnp.where(valid, 0.0, -1e30).astype(jnp.float32)
        own = attend(bias, [queries[b] for b in pair], arrays, plan, kvl, deps)
        if paired:
            results.append((pair, own, swapped(own, "head")))
        else:
            for i, b in enumerate(pair):
                outs[b] = own[i * BLOCK : (i + 1) * BLOCK]
        return (own,)

    def together(i):
        b, n = runs[i]
        return tuple(range(b, b + n))

    deps = keys_values(0, deps)
    deps = all_queries(0, deps)
    deps = keys_values(1, deps)
    deps = all_queries(1, deps)
    deps = keys_values(2, deps)
    deps = attention(together(0), deps)
    deps = all_queries(2, deps)
    deps = keys_values(3, deps)
    deps = all_queries(3, deps)
    deps = attention(together(2), deps)
    deps = attention(together(1), deps)
    deps = attention(together(3), deps)
    if not paired:
        local = jnp.concatenate([outs[b] for b in range(blocks)], 0)
        return lax.all_gather(local, "head", axis=1, tiled=True)
    shape = (rows, n_head * q_weight.shape[1])
    total = None
    for pair, own, _ in results:
        total = place(total, own, mine, pair, shape)
    for pair, _, other in results:
        total = place(total, other, 1 - mine, pair, shape)
    return total


def solution(mesh):
    return jax.shard_map(
        layer,
        mesh=mesh,
        in_specs=(
            P(("groups", "ctx", "sub"), "head"),
            P("sub", "head"),
            P("sub", "head"),
            P("sub", "head"),
            P("head"),
            P("head"),
        ),
        out_specs=P(("groups", "ctx", "sub"), None),
        check_vma=False,
    )
```

```python
import functools
import math

import jax
import jax.numpy as jnp
from jax import lax
from jax.experimental import pallas as pl
from jax.experimental.pallas import tpu as pltpu
from jax.sharding import PartitionSpec as P


HQ = 28
KVH = 4
HD = 128
BLOCK = 128
NEAR = (0, 1, 2, 4)
GROUP = HQ // KVH
SHARED = 4


def shifted(value, axis, steps):
    count = lax.axis_size(axis)
    return lax.ppermute(value, axis, [(s, (s + steps) % count) for s in range(count)])


def swapped(value, axis):
    return lax.ppermute(value, axis, [(0, 1), (1, 0)])


def rotary_tables(positions):
    half = HD // 2
    freqs = jnp.exp(-(2.0 * jnp.arange(half, dtype=jnp.float32) / (2 * half)) * math.log(1000000.0))
    angle = positions[:, None] * freqs[None, :]
    cosine = jnp.cos(angle)
    sine = jnp.sin(angle)
    return jnp.concatenate([cosine, cosine], 1), jnp.concatenate([-sine, sine], 1)


VMEM = pl.BlockSpec(memory_space=pltpu.VMEM)
SMEM = pl.BlockSpec(memory_space=pltpu.SMEM)
ANY = pl.BlockSpec(memory_space=pl.ANY)
HBM = pl.BlockSpec(memory_space=pltpu.HBM)


def params(mib):
    return pltpu.CompilerParams(vmem_limit_bytes=mib * 2**20)


def stage_body(n, flag, *refs):
    own, other, outs, sems = refs[:n], refs[n : 2 * n], refs[-5:-1], refs[-1]

    def bring(first, second):
        copies = []
        for half, sources in enumerate((first, second)):
            q_out, kv_out = outs[2 * half], outs[2 * half + 1]
            nk = sources[1].shape[1]
            targets = (q_out, kv_out.at[:, pl.ds(0, nk)], kv_out.at[:, pl.ds(nk, nk)])
            for i, (source, target) in enumerate(zip(sources, targets)):
                copies.append(pltpu.make_async_copy(source, target, sems.at[half, i]))
        for copy in copies:
            copy.start()
        for copy in copies:
            copy.wait()

    @pl.when(flag[0] == 1)
    def _():
        bring(own, other)

    @pl.when(flag[0] != 1)
    def _():
        bring(other, own)


def stage(flag, own, other, deps):
    half, nq = own[0].shape
    nk = own[1].shape[1]
    shapes = [pltpu.VMEM((half, nq), jnp.bfloat16), pltpu.VMEM((half, 2 * nk), jnp.bfloat16)] * 2
    return pl.pallas_call(
        functools.partial(stage_body, len(own)),
        out_shape=tuple(shapes),
        in_specs=[SMEM] + [HBM] * (2 * len(own)) + [ANY] * len(deps),
        out_specs=(VMEM,) * 4,
        scratch_shapes=[pltpu.SemaphoreType.DMA((2, len(own)))],
        compiler_params=params(2),
        cost_estimate=pl.CostEstimate(flops=0, bytes_accessed=4 * half * (nq + 2 * nk), transcendentals=0),
        name="stage",
    )(flag, *own, *other, *deps)


def project_body(row, tile, rot, ta, tb, wa, wb, bias, cos, sin, *refs):
    out = refs[-1]
    rows = tb.shape[0]
    mine = pl.ds(row, rows)

    def columns(i):
        at = pl.ds(pl.multiple_of(i * tile, tile), tile)
        acc = jnp.dot(ta[mine, :], wa[:, at], preferred_element_type=jnp.float32)
        acc = acc + jnp.dot(tb[...], wb[:, at], preferred_element_type=jnp.float32)
        acc = acc + bias[:, at]
        heads = []
        for h in range(tile // HD):
            v = acc[:, h * HD : (h + 1) * HD]
            if h < rot:
                v = v * cos[mine, :] + pltpu.roll(v, HD // 2, 1) * sin[mine, :]
            heads.append(v.astype(jnp.bfloat16))
        out[:, at] = jnp.concatenate(heads, 1)

    if tile == out.shape[1]:
        columns(0)
    else:
        pl.loop(0, out.shape[1] // tile)(columns)


def project(tokens, row, piece, wa, wb, bias, cos, sin, tile, rot, deps):
    rows, half = piece.shape
    cols = wa.shape[1]
    return pl.pallas_call(
        functools.partial(project_body, row, tile, rot),
        out_shape=jax.ShapeDtypeStruct((rows, cols), jnp.bfloat16),
        in_specs=[VMEM] * 7 + [ANY] * len(deps),
        out_specs=VMEM,
        compiler_params=params(5),
        cost_estimate=pl.CostEstimate(flops=4 * rows * half * cols, bytes_accessed=0, transcendentals=0),
    )(tokens, piece, wa, wb, bias, cos, sin, *deps)


def attend_body(plan, n_arrays, q_row, groups, per, v_base, n_sent, bias, query, *refs):
    arrays = refs[:n_arrays]
    held = refs[-1]
    outs = refs[n_arrays:-1][-2:] if n_sent < groups * per else refs[-2:-1]
    scale = math.log2(math.e) / math.sqrt(HD)
    lower = lax.broadcasted_iota(jnp.int32, (BLOCK, BLOCK), 0) >= lax.broadcasted_iota(
        jnp.int32, (BLOCK, BLOCK), 1
    )
    rows = lambda r: slice(r * BLOCK, (r + 1) * BLOCK)

    def kv_head(g):
        for j, slots in enumerate(plan):
            n = len(slots)
            k_at = pl.ds(pl.multiple_of(g * HD, HD), HD)
            v_at = pl.ds(pl.multiple_of(v_base + g * HD, HD), HD)
            keys = jnp.concatenate([arrays[a][rows(r), k_at] for a, r in slots], 0)
            vals = jnp.concatenate([arrays[a][rows(r), v_at] for a, r in slots], 0)
            vals = jnp.concatenate([vals, jnp.ones_like(vals)], 1)
            for h in range(per):
                at = pl.ds(pl.multiple_of((g * per + h) * HD, HD), HD)
                s = lax.dot_general(
                    query[rows(q_row + j), at], keys, (((1,), (1,)), ((), ())),
                    preferred_element_type=jnp.float32,
                )
                parts = [jnp.where(lower, s[:, :BLOCK], -1e30)]
                for t in range(1, n):
                    parts.append(s[:, t * BLOCK : (t + 1) * BLOCK] + bias[j * n + t])
                s = jnp.concatenate(parts, 1)
                peak = jnp.max(s, axis=1, keepdims=True)
                p = jnp.exp2((s - peak) * scale).astype(jnp.bfloat16)
                o = jnp.dot(p, vals, preferred_element_type=jnp.float32)
                held[rows(j), at] = (o[:, :HD] / o[:, HD:]).astype(jnp.bfloat16)

    if groups == 1:
        kv_head(0)
    else:
        pl.loop(0, groups)(kv_head)
    outs[0][...] = held[:, : n_sent * HD]
    if len(outs) > 1:
        outs[1][...] = held[:, n_sent * HD :]


def attend(bias, query, q_row, arrays, plan, groups, per, v_base, n_sent, deps):
    nb = len(plan)
    heads = groups * per
    keys = len(plan[0]) * BLOCK
    shapes = [jax.ShapeDtypeStruct((nb * BLOCK, n * HD), jnp.bfloat16) for n in (n_sent, heads - n_sent) if n]
    return pl.pallas_call(
        functools.partial(attend_body, plan, len(arrays), q_row, groups, per, v_base, n_sent),
        out_shape=tuple(shapes),
        in_specs=[SMEM] + [VMEM] * (1 + len(arrays)) + [ANY] * len(deps),
        out_specs=(VMEM,) * len(shapes),
        scratch_shapes=[pltpu.VMEM((nb * BLOCK, heads * HD), jnp.bfloat16)],
        compiler_params=params(5),
        cost_estimate=pl.CostEstimate(
            flops=4 * nb * heads * HD * keys * BLOCK,
            bytes_accessed=0,
            transcendentals=nb * BLOCK * heads * keys,
        ),
        name="attend",
    )(bias, query, *arrays, *deps)


def order_body(flag, own, other, first, second, sems):
    def bring(sources):
        copies = [
            pltpu.make_async_copy(source, target, sems.at[i])
            for i, (source, target) in enumerate(zip(sources, (first, second)))
        ]
        for copy in copies:
            copy.start()
        for copy in copies:
            copy.wait()

    @pl.when(flag[0] == 1)
    def _():
        bring((own, other))

    @pl.when(flag[0] != 1)
    def _():
        bring((other, own))


def order_halves(flag, own, other, deps):
    half = pltpu.VMEM(own.shape, own.dtype)
    return pl.pallas_call(
        lambda *refs: order_body(*refs[:3], *refs[-3:]),
        out_shape=(half, half),
        in_specs=[SMEM] + [HBM] * 2 + [ANY] * len(deps),
        out_specs=(VMEM, VMEM),
        scratch_shapes=[pltpu.SemaphoreType.DMA((2,))],
        compiler_params=params(2),
        cost_estimate=pl.CostEstimate(flops=0, bytes_accessed=4 * own.size, transcendentals=0),
        name="order_halves",
    )(flag, own, other, *deps)


def project_shared_body(bases, ta, *refs):
    n_pieces = len(bases)
    pieces = refs[:n_pieces]
    wa, wb, bias, cos, sin = refs[n_pieces : n_pieces + 5]
    out, kv_out = refs[-2:]
    rows = pieces[0].shape[0]
    for i, tb in enumerate(pieces):
        mine = slice(bases[i], bases[i] + rows)
        here = slice(i * rows, (i + 1) * rows)

        def columns(t, last):
            at = pl.ds(pl.multiple_of(t * 2 * HD, 2 * HD), 2 * HD)
            acc = jnp.dot(ta[mine, :], wa[:, at], preferred_element_type=jnp.float32)
            acc = acc + jnp.dot(tb[...], wb[:, at], preferred_element_type=jnp.float32)
            acc = acc + bias[:, at]
            heads = []
            for h in range(2):
                v = acc[:, h * HD : (h + 1) * HD]
                if not (last and h):
                    v = v * cos[mine, :] + pltpu.roll(v, HD // 2, 1) * sin[mine, :]
                heads.append(v.astype(jnp.bfloat16))
            return jnp.concatenate(heads, 1)

        for t in range(SHARED // 2):
            out[here, t * 2 * HD : (t + 1) * 2 * HD] = columns(t, False)
        kv_out[here, :] = columns(SHARED // 2, True)


def project_shared(tokens, bases, pieces, wa, wb, bias, cos, sin, deps):
    rows, half = pieces[0].shape
    total = rows * len(pieces)
    cols = wa.shape[1]
    return pl.pallas_call(
        functools.partial(project_shared_body, bases),
        out_shape=(
            jax.ShapeDtypeStruct((total, SHARED * HD), jnp.bfloat16),
            jax.ShapeDtypeStruct((total, 2 * HD), jnp.bfloat16),
        ),
        in_specs=[VMEM] * (len(pieces) + 6) + [ANY] * len(deps),
        out_specs=(VMEM, VMEM),
        compiler_params=params(5),
        cost_estimate=pl.CostEstimate(flops=4 * total * half * cols, bytes_accessed=0, transcendentals=0),
        name="project_shared",
    )(tokens, *pieces, wa, wb, bias, cos, sin, *deps)


def cut_weights_body(index, wq, wk, wv, out, sems):
    n = out.shape[0]
    rows = pl.ds(pl.multiple_of(index[0] * n, 16), n)
    width = SHARED * HD
    copies = [
        pltpu.make_async_copy(
            wq.at[rows, pl.ds(wq.shape[1] - width, width)], out.at[:, pl.ds(0, width)], sems.at[0]
        ),
        pltpu.make_async_copy(
            wk.at[rows, pl.ds(wk.shape[1] - HD, HD)], out.at[:, pl.ds(width, HD)], sems.at[1]
        ),
        pltpu.make_async_copy(
            wv.at[rows, pl.ds(wv.shape[1] - HD, HD)], out.at[:, pl.ds(width + HD, HD)], sems.at[2]
        ),
    ]
    for copy in copies:
        copy.start()
    for copy in copies:
        copy.wait()


def cut_weights(index, weights, parts):
    n = weights[0].shape[0] // parts
    cols = (SHARED + 2) * HD
    return pl.pallas_call(
        cut_weights_body,
        out_shape=pltpu.VMEM((n, cols), jnp.bfloat16),
        in_specs=[SMEM] + [HBM] * 3,
        out_specs=VMEM,
        scratch_shapes=[pltpu.SemaphoreType.DMA((3,))],
        compiler_params=params(2),
        cost_estimate=pl.CostEstimate(flops=0, bytes_accessed=4 * n * cols, transcendentals=0),
        name="cut_weights",
    )(index, *weights)


def gather_body(n, order, *refs):
    pieces, out, sems = refs[:n], refs[-2], refs[-1]
    rows = pieces[0].shape[0]
    copies = []
    for i, piece in enumerate(pieces):
        at = pl.ds(pl.multiple_of(order[i] * rows, 16), rows)
        copies.append(pltpu.make_async_copy(piece, out.at[at, :], sems.at[i]))
    for copy in copies:
        copy.start()
    for copy in copies:
        copy.wait()


def gather(order, pieces, deps):
    rows, cols = pieces[0].shape
    return pl.pallas_call(
        functools.partial(gather_body, len(pieces)),
        out_shape=pltpu.VMEM((rows * len(pieces), cols), jnp.bfloat16),
        in_specs=[SMEM] + [ANY] * (len(pieces) + len(deps)),
        out_specs=VMEM,
        scratch_shapes=[pltpu.SemaphoreType.DMA((len(pieces),))],
        compiler_params=params(6),
        cost_estimate=pl.CostEstimate(
            flops=0, bytes_accessed=4 * rows * cols * len(pieces), transcendentals=0
        ),
        name="gather",
    )(order, *pieces, *deps)


def cut_body(row, source, out, sem):
    copy = pltpu.make_async_copy(source.at[pl.ds(row, out.shape[0]), :], out, sem)
    copy.start()
    copy.wait()


def cut(source, block, count):
    return pl.pallas_call(
        functools.partial(cut_body, block * BLOCK),
        out_shape=pltpu.VMEM((count * BLOCK, source.shape[1]), source.dtype),
        in_specs=[HBM],
        out_specs=VMEM,
        scratch_shapes=[pltpu.SemaphoreType.DMA],
        compiler_params=params(2),
        cost_estimate=pl.CostEstimate(
            flops=0, bytes_accessed=2 * count * BLOCK * source.shape[1], transcendentals=0
        ),
        name="cut",
    )(source)


def place_body(items, sides, *refs):
    out, sems = refs[-2:]
    copies = []
    for i, (first, side) in enumerate(items):
        rows, cols = refs[i].shape
        at = pl.ds(pl.multiple_of(sides[side] * HD, HD), cols)
        copies.append(
            pltpu.make_async_copy(refs[i], out.at[pl.ds(first * BLOCK, rows), at], sems.at[i])
        )
    for copy in copies:
        copy.start()
    for copy in copies:
        copy.wait()


def place(total, sides, items, shape, deps=()):
    arrays = [array for array, _, _ in items]
    rest = list(deps) if total is None else [*deps, total]
    aliases = {} if total is None else {len(arrays) + len(rest): 0}
    return pl.pallas_call(
        functools.partial(place_body, [(first, side) for _, first, side in items]),
        out_shape=jax.ShapeDtypeStruct(shape, jnp.bfloat16),
        in_specs=[SMEM] + [VMEM] * len(arrays) + [ANY] * len(deps) + ([] if total is None else [HBM]),
        out_specs=HBM,
        scratch_shapes=[pltpu.SemaphoreType.DMA((len(arrays),))],
        input_output_aliases=aliases,
        compiler_params=params(8),
        cost_estimate=pl.CostEstimate(
            flops=0, bytes_accessed=4 * sum(a.size for a in arrays), transcendentals=0
        ),
        name="place",
    )(sides, *arrays, *rest)


def chunks_of(blocks):
    n = blocks // 4
    return [(quarter * n, n) for quarter in (2, 0, 1, 3)]


def layer(tokens, q_weight, k_weight, v_weight, q_bias, v_bias):
    n_sub = lax.axis_size("sub")
    n_ctx = lax.axis_size("ctx")
    n_head = lax.axis_size("head")
    n_groups = lax.axis_size("groups")
    rows = tokens.shape[0]
    blocks = rows // BLOCK
    nq = q_weight.shape[1]
    kvl = k_weight.shape[1] // HD
    sub = lax.axis_index("sub")
    ctx = lax.axis_index("ctx")
    head = lax.axis_index("head")
    group = lax.axis_index("groups")
    shard = ctx * n_sub + sub
    runs = chunks_of(blocks)
    weights = (q_weight, k_weight, v_weight)

    paired = n_head == 2 and kvl == 2 and n_groups == 2
    if paired:
        parts = n_groups * n_ctx
        mine = (ctx * n_groups + group).astype(jnp.int32).reshape(1)
        part = cut_weights(mine, weights, parts)
        ring = [swapped(part, "head")]
        pieces = []
        for b, n in runs:
            pieces.append(swapped(cut(tokens, b, n), "head"))
        flag = (sub == head).astype(jnp.int32).reshape(1)
        shared_bias = jnp.concatenate(
            [q_bias[nq - SHARED * HD :], jnp.zeros((HD,), jnp.float32), v_bias[(kvl - 1) * HD :]]
        )[None, :]
        shared_bias = swapped(shared_bias, "head")
        for _ in range(1, n_ctx):
            ring.append(shifted(ring[-1], "ctx", 1))
        across = []
        for d in range(n_ctx):
            across.append(swapped(ring[d], "groups"))
        turn = jnp.arange(2 * n_ctx, dtype=jnp.int32)
        there = lax.rem(ctx + n_ctx - turn % n_ctx, n_ctx) * n_groups
        part_order = jnp.where(turn < n_ctx, there + group, there + 1 - group).astype(jnp.int32)
    else:
        features = lax.all_gather(tokens, "head", axis=1, tiled=True)
        half = features.shape[1] // n_sub
        flag = (sub == 0).astype(jnp.int32).reshape(1)
        tokens = features[:, :half]
        pieces = [features[b * BLOCK : (b + n) * BLOCK, half:] for b, n in runs]
    other = swapped(k_weight, "sub"), swapped(v_weight, "sub")
    other = (swapped(q_weight, "sub"),) + other
    qb = q_bias[None, :]
    kvb = jnp.concatenate([jnp.zeros_like(v_bias), v_bias])[None, :]
    positions = (shard * rows + jnp.arange(rows, dtype=jnp.int32)).astype(jnp.float32)
    cos, sin = rotary_tables(positions)

    far_steps = [s for s in (1, 2, 4, 8) if s < n_ctx]
    biases = []
    for b, n in runs:
        steps = jnp.array(list(NEAR) + [blocks] + [n_sub * blocks * s for s in far_steps], jnp.int32)
        places = shard * blocks + b + jnp.arange(n, dtype=jnp.int32)
        biases.append(jnp.where(places[:, None] >= steps[None, :], 0.0, -1e30).astype(jnp.float32).reshape(-1))
    small = [qb, kvb, cos, sin, *biases]
    if paired:
        columns = kvl * GROUP
        sides = columns * jnp.array([0, 1, 1, 2], jnp.int32) - SHARED * jnp.array([0, 1, 0, 1], jnp.int32)
        sides = sides + head.astype(jnp.int32) * columns * jnp.array([1, 1, -1, -1], jnp.int32)
        small += [sides, part_order]
    wqa, wkva, wqb, wkvb = stage(flag, weights, other, small)
    queries, sources = {}, {}
    shared_queries, shared_sources = {}, {}

    def exchanged(kv, places, table):
        held = {"own": kv}
        held["prev"] = shifted(kv, ("ctx", "sub"), 1)
        for s in far_steps:
            held["far", s] = shifted(kv, "ctx", 1) if s == 1 else shifted(held["far", s // 2], "ctx", s // 2)
        for r, b in enumerate(places):
            for name, array in held.items():
                table[name, b] = (array, r)

    def keys_values(i, deps):
        (b, n), piece = runs[i], pieces[i]
        kv = project(tokens, b * BLOCK, piece, wkva, wkvb, kvb, cos, sin, 2 * kvl * HD, kvl, deps)
        exchanged(kv, range(b, b + n), sources)
        return (kv,)

    def all_queries(i, deps):
        (b, n), piece = runs[i], pieces[i]
        tile = 2 * HD if nq % (2 * HD) == 0 else HD
        q = project(tokens, b * BLOCK, piece, wqa, wqb, qb, cos, sin, tile, tile // HD, deps)
        for r in range(n):
            queries[b + r] = (q, r)
        return (q,)

    def neighbours_head(which, deps):
        bases = [runs[i][0] * BLOCK for i in which]
        qkv, kv = project_shared(
            tokens, bases, [pieces[i] for i in which], *shared_weights, shared_bias, cos, sin, deps
        )
        exchanged(kv, [b for i in which for b in range(runs[i][0], sum(runs[i]))], shared_sources)
        r = 0
        for i in which:
            for b in range(runs[i][0], sum(runs[i])):
                shared_queries[b] = (qkv, r)
                r += 1
        return (kv,)

    def attention(i, kind, deps):
        b0, count = runs[i]
        pair = tuple(range(b0, b0 + count))
        if kind == "neighbour":
            qs, table, form = shared_queries, shared_sources, (1, SHARED, HD, SHARED)
        else:
            n_sent = kvl * GROUP - (SHARED if paired else 0)
            qs, table, form = queries, sources, (kvl, GROUP, kvl * HD, n_sent)
        arrays, plan = [], []
        for b in pair:
            slots = []
            wanted = [(d, ("own", b - d) if d <= b else ("prev", blocks + b - d)) for d in NEAR + (blocks,)]
            wanted += [(n_sub * blocks * s, (("far", s), b)) for s in far_steps]
            for d, key in wanted:
                array, r = table[key]
                at = next((k for k, a in enumerate(arrays) if a is array), None)
                if at is None:
                    at = len(arrays)
                    arrays.append(array)
                slots.append((at, r))
            plan.append(tuple(slots))
        return attend(biases[i], *qs[b0], arrays, plan, *form, deps)

    shape = (rows, n_head * nq)
    if not paired:
        deps = ()
        for i in range(len(runs)):
            deps = keys_values(i, deps)
            deps = all_queries(i, deps)
        outs = {}
        for i, (b, _) in enumerate(runs):
            outs[b] = attention(i, "own", deps)[0]
        local = jnp.concatenate([outs[b] for b in sorted(outs)], 0)
        return lax.all_gather(local, "head", axis=1, tiled=True)

    sent, received, kept, extra = {}, {}, {}, {}

    def send(i, deps):
        sent[i], kept[i] = attention(i, "own", deps)
        received[i] = swapped(sent[i], "head")
        return (kept[i],)

    def add(i, deps):
        extra[i] = attention(i, "neighbour", deps)[0]
        return (extra[i],)

    deps = (wqa,)
    deps = keys_values(0, deps)
    deps = all_queries(0, deps)
    deps = keys_values(1, deps)
    deps = all_queries(1, deps)
    gathered = gather(part_order, ring + across, deps)
    shared_other = swapped(gathered, "sub")
    shared_weights = order_halves(flag, gathered, shared_other, (gathered,))
    deps = neighbours_head((0, 1), (shared_weights[0],))
    deps = keys_values(2, deps)
    deps = send(0, deps)
    deps = keys_values(3, deps)
    deps = all_queries(2, deps)
    deps = send(1, deps)
    deps = send(2, deps)
    deps = neighbours_head((2, 3), deps)
    deps = all_queries(3, deps)
    deps = send(3, deps)
    deps = add(0, deps)
    deps = add(1, deps)
    deps = add(2, deps)
    deps = add(3, deps)
    first = lambda i: runs[i][0]
    total = place(
        None, sides,
        [(sent[i], first(i), 0) for i in range(4)] + [(kept[i], first(i), 1) for i in range(4)]
        + [(extra[i], first(i), 3) for i in range(4)],
        shape,
    )
    total = place(total, sides, [(received[i], first(i), 2) for i in (0, 1)], shape)
    total = place(total, sides, [(received[2], first(2), 2)], shape)
    return place(total, sides, [(received[3], first(3), 2)], shape)


def solution(mesh):
    return jax.shard_map(
        layer,
        mesh=mesh,
        in_specs=(
            P(("groups", "ctx", "sub"), "head"),
            P("sub", "head"),
            P("sub", "head"),
            P("sub", "head"),
            P("head"),
            P("head"),
        ),
        out_specs=P(("groups", "ctx", "sub"), None),
        check_vma=False,
    )
```

```python
import functools
import math

import jax
import jax.numpy as jnp
from jax import lax
from jax.experimental import pallas as pl
from jax.experimental.pallas import tpu as pltpu
from jax.sharding import PartitionSpec as P


HQ = 28
KVH = 4
HD = 128
BLOCK = 128
NEAR = (0, 1, 2, 4)
GROUP = HQ // KVH
SHARED = 4


def shifted(value, axis, steps):
    count = lax.axis_size(axis)
    return lax.ppermute(value, axis, [(s, (s + steps) % count) for s in range(count)])


def swapped(value, axis):
    return lax.ppermute(value, axis, [(0, 1), (1, 0)])


def rotary_tables(positions):
    half = HD // 2
    freqs = jnp.exp(-(2.0 * jnp.arange(half, dtype=jnp.float32) / (2 * half)) * math.log(1000000.0))
    angle = positions[:, None] * freqs[None, :]
    cosine = jnp.cos(angle)
    sine = jnp.sin(angle)
    return jnp.concatenate([cosine, cosine], 1), jnp.concatenate([-sine, sine], 1)


VMEM = pl.BlockSpec(memory_space=pltpu.VMEM)
SMEM = pl.BlockSpec(memory_space=pltpu.SMEM)
ANY = pl.BlockSpec(memory_space=pl.ANY)
HBM = pl.BlockSpec(memory_space=pltpu.HBM)


def params(mib):
    return pltpu.CompilerParams(vmem_limit_bytes=mib * 2**20)


def stage_body(n, flag, *refs):
    own, other, outs, sems = refs[:n], refs[n : 2 * n], refs[-5:-1], refs[-1]

    def bring(first, second):
        copies = []
        for half, sources in enumerate((first, second)):
            q_out, kv_out = outs[2 * half], outs[2 * half + 1]
            nk = sources[1].shape[1]
            targets = (q_out, kv_out.at[:, pl.ds(0, nk)], kv_out.at[:, pl.ds(nk, nk)])
            for i, (source, target) in enumerate(zip(sources, targets)):
                copies.append(pltpu.make_async_copy(source, target, sems.at[half, i]))
        for copy in copies:
            copy.start()
        for copy in copies:
            copy.wait()

    @pl.when(flag[0] == 1)
    def _():
        bring(own, other)

    @pl.when(flag[0] != 1)
    def _():
        bring(other, own)


def stage(flag, own, other, deps):
    half, nq = own[0].shape
    nk = own[1].shape[1]
    shapes = [pltpu.VMEM((half, nq), jnp.bfloat16), pltpu.VMEM((half, 2 * nk), jnp.bfloat16)] * 2
    return pl.pallas_call(
        functools.partial(stage_body, len(own)),
        out_shape=tuple(shapes),
        in_specs=[SMEM] + [HBM] * (2 * len(own)) + [ANY] * len(deps),
        out_specs=(VMEM,) * 4,
        scratch_shapes=[pltpu.SemaphoreType.DMA((2, len(own)))],
        compiler_params=params(2),
        cost_estimate=pl.CostEstimate(flops=0, bytes_accessed=4 * half * (nq + 2 * nk), transcendentals=0),
        name="stage",
    )(flag, *own, *other, *deps)


def project_body(row, tile, rot, ta, tb, wa, wb, bias, cos, sin, *refs):
    out = refs[-1]
    rows = tb.shape[0]
    mine = pl.ds(row, rows)

    def columns(i):
        at = pl.ds(pl.multiple_of(i * tile, tile), tile)
        acc = jnp.dot(ta[mine, :], wa[:, at], preferred_element_type=jnp.float32)
        acc = acc + jnp.dot(tb[...], wb[:, at], preferred_element_type=jnp.float32)
        acc = acc + bias[:, at]
        heads = []
        for h in range(tile // HD):
            v = acc[:, h * HD : (h + 1) * HD]
            if h < rot:
                v = v * cos[mine, :] + pltpu.roll(v, HD // 2, 1) * sin[mine, :]
            heads.append(v.astype(jnp.bfloat16))
        out[:, at] = jnp.concatenate(heads, 1)

    if tile == out.shape[1]:
        columns(0)
    else:
        pl.loop(0, out.shape[1] // tile)(columns)


def project(tokens, row, piece, wa, wb, bias, cos, sin, tile, rot, deps):
    rows, half = piece.shape
    cols = wa.shape[1]
    return pl.pallas_call(
        functools.partial(project_body, row, tile, rot),
        out_shape=jax.ShapeDtypeStruct((rows, cols), jnp.bfloat16),
        in_specs=[VMEM] * 7 + [ANY] * len(deps),
        out_specs=VMEM,
        compiler_params=params(5),
        cost_estimate=pl.CostEstimate(flops=4 * rows * half * cols, bytes_accessed=0, transcendentals=0),
    )(tokens, piece, wa, wb, bias, cos, sin, *deps)


def attend_body(plan, n_arrays, q_row, groups, per, v_base, n_sent, bias, query, *refs):
    arrays = refs[:n_arrays]
    held = refs[-1]
    outs = refs[n_arrays:-1][-2:] if n_sent < groups * per else refs[-2:-1]
    scale = math.log2(math.e) / math.sqrt(HD)
    lower = lax.broadcasted_iota(jnp.int32, (BLOCK, BLOCK), 0) >= lax.broadcasted_iota(
        jnp.int32, (BLOCK, BLOCK), 1
    )
    rows = lambda r: slice(r * BLOCK, (r + 1) * BLOCK)

    def kv_head(g):
        for j, slots in enumerate(plan):
            n = len(slots)
            k_at = pl.ds(pl.multiple_of(g * HD, HD), HD)
            v_at = pl.ds(pl.multiple_of(v_base + g * HD, HD), HD)
            keys = jnp.concatenate([arrays[a][rows(r), k_at] for a, r in slots], 0)
            vals = jnp.concatenate([arrays[a][rows(r), v_at] for a, r in slots], 0)
            vals = jnp.concatenate([vals, jnp.ones_like(vals)], 1)
            for h in range(per):
                at = pl.ds(pl.multiple_of((g * per + h) * HD, HD), HD)
                s = lax.dot_general(
                    query[rows(q_row + j), at], keys, (((1,), (1,)), ((), ())),
                    preferred_element_type=jnp.float32,
                )
                parts = [jnp.where(lower, s[:, :BLOCK], -1e30)]
                for t in range(1, n):
                    parts.append(s[:, t * BLOCK : (t + 1) * BLOCK] + bias[j * n + t])
                s = jnp.concatenate(parts, 1)
                peak = jnp.max(s, axis=1, keepdims=True)
                p = jnp.exp2((s - peak) * scale).astype(jnp.bfloat16)
                o = jnp.dot(p, vals, preferred_element_type=jnp.float32)
                held[rows(j), at] = (o[:, :HD] / o[:, HD:]).astype(jnp.bfloat16)

    if groups == 1:
        kv_head(0)
    else:
        pl.loop(0, groups)(kv_head)
    outs[0][...] = held[:, : n_sent * HD]
    if len(outs) > 1:
        outs[1][...] = held[:, n_sent * HD :]


def attend(bias, query, q_row, arrays, plan, groups, per, v_base, n_sent, deps):
    nb = len(plan)
    heads = groups * per
    keys = len(plan[0]) * BLOCK
    shapes = [jax.ShapeDtypeStruct((nb * BLOCK, n * HD), jnp.bfloat16) for n in (n_sent, heads - n_sent) if n]
    return pl.pallas_call(
        functools.partial(attend_body, plan, len(arrays), q_row, groups, per, v_base, n_sent),
        out_shape=tuple(shapes),
        in_specs=[SMEM] + [VMEM] * (1 + len(arrays)) + [ANY] * len(deps),
        out_specs=(VMEM,) * len(shapes),
        scratch_shapes=[pltpu.VMEM((nb * BLOCK, heads * HD), jnp.bfloat16)],
        compiler_params=params(5),
        cost_estimate=pl.CostEstimate(
            flops=4 * nb * heads * HD * keys * BLOCK,
            bytes_accessed=0,
            transcendentals=nb * BLOCK * heads * keys,
        ),
        name="attend",
    )(bias, query, *arrays, *deps)


def order_body(flag, own, other, first, second, sems):
    def bring(sources):
        copies = [
            pltpu.make_async_copy(source, target, sems.at[i])
            for i, (source, target) in enumerate(zip(sources, (first, second)))
        ]
        for copy in copies:
            copy.start()
        for copy in copies:
            copy.wait()

    @pl.when(flag[0] == 1)
    def _():
        bring((own, other))

    @pl.when(flag[0] != 1)
    def _():
        bring((other, own))


def order_halves(flag, own, other, deps):
    half = pltpu.VMEM(own.shape, own.dtype)
    return pl.pallas_call(
        lambda *refs: order_body(*refs[:3], *refs[-3:]),
        out_shape=(half, half),
        in_specs=[SMEM] + [HBM] * 2 + [ANY] * len(deps),
        out_specs=(VMEM, VMEM),
        scratch_shapes=[pltpu.SemaphoreType.DMA((2,))],
        compiler_params=params(2),
        cost_estimate=pl.CostEstimate(flops=0, bytes_accessed=4 * own.size, transcendentals=0),
        name="order_halves",
    )(flag, own, other, *deps)


def project_shared_body(bases, ta, *refs):
    n_pieces = len(bases)
    pieces = refs[:n_pieces]
    wa, wb, bias, cos, sin = refs[n_pieces : n_pieces + 5]
    out, kv_out = refs[-2:]
    rows = pieces[0].shape[0]
    for i, tb in enumerate(pieces):
        mine = slice(bases[i], bases[i] + rows)
        here = slice(i * rows, (i + 1) * rows)

        def columns(t, last):
            at = pl.ds(pl.multiple_of(t * 2 * HD, 2 * HD), 2 * HD)
            acc = jnp.dot(ta[mine, :], wa[:, at], preferred_element_type=jnp.float32)
            acc = acc + jnp.dot(tb[...], wb[:, at], preferred_element_type=jnp.float32)
            acc = acc + bias[:, at]
            heads = []
            for h in range(2):
                v = acc[:, h * HD : (h + 1) * HD]
                if not (last and h):
                    v = v * cos[mine, :] + pltpu.roll(v, HD // 2, 1) * sin[mine, :]
                heads.append(v.astype(jnp.bfloat16))
            return jnp.concatenate(heads, 1)

        for t in range(SHARED // 2):
            out[here, t * 2 * HD : (t + 1) * 2 * HD] = columns(t, False)
        kv_out[here, :] = columns(SHARED // 2, True)


def project_shared(tokens, bases, pieces, wa, wb, bias, cos, sin, deps):
    rows, half = pieces[0].shape
    total = rows * len(pieces)
    cols = wa.shape[1]
    return pl.pallas_call(
        functools.partial(project_shared_body, bases),
        out_shape=(
            jax.ShapeDtypeStruct((total, SHARED * HD), jnp.bfloat16),
            jax.ShapeDtypeStruct((total, 2 * HD), jnp.bfloat16),
        ),
        in_specs=[VMEM] * (len(pieces) + 6) + [ANY] * len(deps),
        out_specs=(VMEM, VMEM),
        compiler_params=params(5),
        cost_estimate=pl.CostEstimate(flops=4 * total * half * cols, bytes_accessed=0, transcendentals=0),
        name="project_shared",
    )(tokens, *pieces, wa, wb, bias, cos, sin, *deps)


def cut_weights_body(index, wq, wk, wv, out, sems):
    n = out.shape[0]
    rows = pl.ds(pl.multiple_of(index[0] * n, 16), n)
    width = SHARED * HD
    copies = [
        pltpu.make_async_copy(
            wq.at[rows, pl.ds(wq.shape[1] - width, width)], out.at[:, pl.ds(0, width)], sems.at[0]
        ),
        pltpu.make_async_copy(
            wk.at[rows, pl.ds(wk.shape[1] - HD, HD)], out.at[:, pl.ds(width, HD)], sems.at[1]
        ),
        pltpu.make_async_copy(
            wv.at[rows, pl.ds(wv.shape[1] - HD, HD)], out.at[:, pl.ds(width + HD, HD)], sems.at[2]
        ),
    ]
    for copy in copies:
        copy.start()
    for copy in copies:
        copy.wait()


def cut_weights(index, weights, parts):
    n = weights[0].shape[0] // parts
    cols = (SHARED + 2) * HD
    return pl.pallas_call(
        cut_weights_body,
        out_shape=pltpu.VMEM((n, cols), jnp.bfloat16),
        in_specs=[SMEM] + [HBM] * 3,
        out_specs=VMEM,
        scratch_shapes=[pltpu.SemaphoreType.DMA((3,))],
        compiler_params=params(2),
        cost_estimate=pl.CostEstimate(flops=0, bytes_accessed=4 * n * cols, transcendentals=0),
        name="cut_weights",
    )(index, *weights)


def gather_body(n, order, *refs):
    pieces, out, sems = refs[:n], refs[-2], refs[-1]
    rows = pieces[0].shape[0]
    copies = []
    for i, piece in enumerate(pieces):
        at = pl.ds(pl.multiple_of(order[i] * rows, 16), rows)
        copies.append(pltpu.make_async_copy(piece, out.at[at, :], sems.at[i]))
    for copy in copies:
        copy.start()
    for copy in copies:
        copy.wait()


def gather(order, pieces, deps):
    rows, cols = pieces[0].shape
    return pl.pallas_call(
        functools.partial(gather_body, len(pieces)),
        out_shape=pltpu.VMEM((rows * len(pieces), cols), jnp.bfloat16),
        in_specs=[SMEM] + [ANY] * (len(pieces) + len(deps)),
        out_specs=VMEM,
        scratch_shapes=[pltpu.SemaphoreType.DMA((len(pieces),))],
        compiler_params=params(6),
        cost_estimate=pl.CostEstimate(
            flops=0, bytes_accessed=4 * rows * cols * len(pieces), transcendentals=0
        ),
        name="gather",
    )(order, *pieces, *deps)


def cut_body(row, source, out, sem):
    copy = pltpu.make_async_copy(source.at[pl.ds(row, out.shape[0]), :], out, sem)
    copy.start()
    copy.wait()


def cut(source, block, count):
    return pl.pallas_call(
        functools.partial(cut_body, block * BLOCK),
        out_shape=pltpu.VMEM((count * BLOCK, source.shape[1]), source.dtype),
        in_specs=[HBM],
        out_specs=VMEM,
        scratch_shapes=[pltpu.SemaphoreType.DMA],
        compiler_params=params(2),
        cost_estimate=pl.CostEstimate(
            flops=0, bytes_accessed=2 * count * BLOCK * source.shape[1], transcendentals=0
        ),
        name="cut",
    )(source)


def place_body(items, sides, *refs):
    out, sems = refs[-2:]
    copies = []
    for i, (first, side) in enumerate(items):
        rows, cols = refs[i].shape
        at = pl.ds(pl.multiple_of(sides[side] * HD, HD), cols)
        copies.append(
            pltpu.make_async_copy(refs[i], out.at[pl.ds(first * BLOCK, rows), at], sems.at[i])
        )
    for copy in copies:
        copy.start()
    for copy in copies:
        copy.wait()


def place(total, sides, items, shape, deps=()):
    arrays = [array for array, _, _ in items]
    rest = list(deps) if total is None else [*deps, total]
    aliases = {} if total is None else {len(arrays) + len(rest): 0}
    return pl.pallas_call(
        functools.partial(place_body, [(first, side) for _, first, side in items]),
        out_shape=jax.ShapeDtypeStruct(shape, jnp.bfloat16),
        in_specs=[SMEM] + [VMEM] * len(arrays) + [ANY] * len(deps) + ([] if total is None else [HBM]),
        out_specs=HBM,
        scratch_shapes=[pltpu.SemaphoreType.DMA((len(arrays),))],
        input_output_aliases=aliases,
        compiler_params=params(3),
        cost_estimate=pl.CostEstimate(
            flops=0, bytes_accessed=4 * sum(a.size for a in arrays), transcendentals=0
        ),
        name="place",
    )(sides, *arrays, *rest)


def chunks_of(blocks):
    n = blocks // 4
    return [(quarter * n, n) for quarter in (2, 0, 1, 3)]


def layer(tokens, q_weight, k_weight, v_weight, q_bias, v_bias):
    n_sub = lax.axis_size("sub")
    n_ctx = lax.axis_size("ctx")
    n_head = lax.axis_size("head")
    n_groups = lax.axis_size("groups")
    rows = tokens.shape[0]
    blocks = rows // BLOCK
    nq = q_weight.shape[1]
    kvl = k_weight.shape[1] // HD
    sub = lax.axis_index("sub")
    ctx = lax.axis_index("ctx")
    head = lax.axis_index("head")
    group = lax.axis_index("groups")
    shard = ctx * n_sub + sub
    runs = chunks_of(blocks)
    weights = (q_weight, k_weight, v_weight)

    paired = n_head == 2 and kvl == 2 and n_groups == 2
    if paired:
        parts = n_groups * n_ctx
        mine = (ctx * n_groups + group).astype(jnp.int32).reshape(1)
        part = cut_weights(mine, weights, parts)
        ring = [swapped(part, "head")]
        pieces = []
        for b, n in runs:
            pieces.append(swapped(cut(tokens, b, n), "head"))
        flag = (sub == head).astype(jnp.int32).reshape(1)
        shared_bias = jnp.concatenate(
            [q_bias[nq - SHARED * HD :], jnp.zeros((HD,), jnp.float32), v_bias[(kvl - 1) * HD :]]
        )[None, :]
        shared_bias = swapped(shared_bias, "head")
        for _ in range(1, n_ctx):
            ring.append(shifted(ring[-1], "ctx", 1))
        across = []
        for d in range(n_ctx):
            across.append(swapped(ring[d], "groups"))
        turn = jnp.arange(2 * n_ctx, dtype=jnp.int32)
        there = lax.rem(ctx + n_ctx - turn % n_ctx, n_ctx) * n_groups
        part_order = jnp.where(turn < n_ctx, there + group, there + 1 - group).astype(jnp.int32)
    else:
        features = lax.all_gather(tokens, "head", axis=1, tiled=True)
        half = features.shape[1] // n_sub
        flag = (sub == 0).astype(jnp.int32).reshape(1)
        tokens = features[:, :half]
        pieces = [features[b * BLOCK : (b + n) * BLOCK, half:] for b, n in runs]
    other = swapped(k_weight, "sub"), swapped(v_weight, "sub")
    other = (swapped(q_weight, "sub"),) + other
    qb = q_bias[None, :]
    kvb = jnp.concatenate([jnp.zeros_like(v_bias), v_bias])[None, :]
    positions = (shard * rows + jnp.arange(rows, dtype=jnp.int32)).astype(jnp.float32)
    cos, sin = rotary_tables(positions)

    far_steps = [s for s in (1, 2, 4, 8) if s < n_ctx]
    biases = []
    for b, n in runs:
        steps = jnp.array(list(NEAR) + [blocks] + [n_sub * blocks * s for s in far_steps], jnp.int32)
        places = shard * blocks + b + jnp.arange(n, dtype=jnp.int32)
        biases.append(jnp.where(places[:, None] >= steps[None, :], 0.0, -1e30).astype(jnp.float32).reshape(-1))
    small = [qb, kvb, cos, sin, *biases]
    if paired:
        columns = kvl * GROUP
        sides = columns * jnp.array([0, 1, 1, 2], jnp.int32) - SHARED * jnp.array([0, 1, 0, 1], jnp.int32)
        sides = sides + head.astype(jnp.int32) * columns * jnp.array([1, 1, -1, -1], jnp.int32)
        small += [sides, part_order]
    wqa, wkva, wqb, wkvb = stage(flag, weights, other, small)
    queries, sources = {}, {}
    shared_queries, shared_sources = {}, {}

    def exchanged(kv, places, table):
        held = {"own": kv}
        held["prev"] = shifted(kv, ("ctx", "sub"), 1)
        for s in far_steps:
            held["far", s] = shifted(kv, "ctx", 1) if s == 1 else shifted(held["far", s // 2], "ctx", s // 2)
        for r, b in enumerate(places):
            for name, array in held.items():
                table[name, b] = (array, r)

    def keys_values(i, deps):
        (b, n), piece = runs[i], pieces[i]
        kv = project(tokens, b * BLOCK, piece, wkva, wkvb, kvb, cos, sin, 2 * kvl * HD, kvl, deps)
        exchanged(kv, range(b, b + n), sources)
        return (kv,)

    def all_queries(i, deps):
        (b, n), piece = runs[i], pieces[i]
        tile = 2 * HD if nq % (2 * HD) == 0 else HD
        q = project(tokens, b * BLOCK, piece, wqa, wqb, qb, cos, sin, tile, tile // HD, deps)
        for r in range(n):
            queries[b + r] = (q, r)
        return (q,)

    def neighbours_head(which, deps):
        bases = [runs[i][0] * BLOCK for i in which]
        qkv, kv = project_shared(
            tokens, bases, [pieces[i] for i in which], *shared_weights, shared_bias, cos, sin, deps
        )
        exchanged(kv, [b for i in which for b in range(runs[i][0], sum(runs[i]))], shared_sources)
        r = 0
        for i in which:
            for b in range(runs[i][0], sum(runs[i])):
                shared_queries[b] = (qkv, r)
                r += 1
        return (kv,)

    def attention(i, kind, deps):
        b0, count = runs[i]
        pair = tuple(range(b0, b0 + count))
        if kind == "neighbour":
            qs, table, form = shared_queries, shared_sources, (1, SHARED, HD, SHARED)
        else:
            n_sent = kvl * GROUP - (SHARED if paired else 0)
            qs, table, form = queries, sources, (kvl, GROUP, kvl * HD, n_sent)
        arrays, plan = [], []
        for b in pair:
            slots = []
            wanted = [(d, ("own", b - d) if d <= b else ("prev", blocks + b - d)) for d in NEAR + (blocks,)]
            wanted += [(n_sub * blocks * s, (("far", s), b)) for s in far_steps]
            for d, key in wanted:
                array, r = table[key]
                at = next((k for k, a in enumerate(arrays) if a is array), None)
                if at is None:
                    at = len(arrays)
                    arrays.append(array)
                slots.append((at, r))
            plan.append(tuple(slots))
        return attend(biases[i], *qs[b0], arrays, plan, *form, deps)

    shape = (rows, n_head * nq)
    if not paired:
        deps = ()
        for i in range(len(runs)):
            deps = keys_values(i, deps)
            deps = all_queries(i, deps)
        outs = {}
        for i, (b, _) in enumerate(runs):
            outs[b] = attention(i, "own", deps)[0]
        local = jnp.concatenate([outs[b] for b in sorted(outs)], 0)
        return lax.all_gather(local, "head", axis=1, tiled=True)

    sent, received, kept, extra = {}, {}, {}, {}

    def send(i, deps):
        sent[i], kept[i] = attention(i, "own", deps)
        received[i] = swapped(sent[i], "head")
        return (kept[i],)

    def add(i, deps):
        extra[i] = attention(i, "neighbour", deps)[0]
        return (extra[i],)

    deps = (wqa,)
    deps = keys_values(0, deps)
    deps = all_queries(0, deps)
    deps = keys_values(1, deps)
    deps = all_queries(1, deps)
    gathered = gather(part_order, ring + across, deps)
    shared_other = swapped(gathered, "sub")
    shared_weights = order_halves(flag, gathered, shared_other, (gathered,))
    deps = neighbours_head((0, 1), (shared_weights[0],))
    deps = keys_values(2, deps)
    deps = send(0, deps)
    deps = all_queries(2, deps)
    deps = keys_values(3, deps)
    deps = neighbours_head((2, 3), deps)
    deps = send(1, deps)
    deps = send(2, deps)
    deps = all_queries(3, deps)
    deps = send(3, deps)
    deps = add(0, deps)
    deps = add(1, deps)
    first = lambda i: runs[i][0]
    total = place(
        None, sides,
        [(sent[i], first(i), 0) for i in range(4)] + [(kept[i], first(i), 1) for i in range(4)]
        + [(extra[i], first(i), 3) for i in (0, 1)],
        shape, deps,
    )
    deps = add(2, deps)
    deps = add(3, deps)
    total = place(
        total, sides,
        [(extra[i], first(i), 3) for i in (2, 3)] + [(received[i], first(i), 2) for i in (0, 1, 2)], shape,
    )
    return place(total, sides, [(received[3], first(3), 2)], shape)


def solution(mesh):
    return jax.shard_map(
        layer,
        mesh=mesh,
        in_specs=(
            P(("groups", "ctx", "sub"), "head"),
            P("sub", "head"),
            P("sub", "head"),
            P("sub", "head"),
            P("head"),
            P("head"),
        ),
        out_specs=P(("groups", "ctx", "sub"), None),
        check_vma=False,
    )
```

```python
import functools
import math

import jax
import jax.numpy as jnp
from jax import lax
from jax.experimental import pallas as pl
from jax.experimental.pallas import tpu as pltpu
from jax.sharding import PartitionSpec as P


HQ = 28
KVH = 4
HD = 128
BLOCK = 128
NEAR = (0, 1, 2, 4)
GROUP = HQ // KVH
SHARED = 4


def shifted(value, axis, steps):
    count = lax.axis_size(axis)
    return lax.ppermute(value, axis, [(s, (s + steps) % count) for s in range(count)])


def swapped(value, axis):
    return lax.ppermute(value, axis, [(0, 1), (1, 0)])


def rotary_tables(positions):
    half = HD // 2
    freqs = jnp.exp(-(2.0 * jnp.arange(half, dtype=jnp.float32) / (2 * half)) * math.log(1000000.0))
    angle = positions[:, None] * freqs[None, :]
    cosine = jnp.cos(angle)
    sine = jnp.sin(angle)
    return jnp.concatenate([cosine, cosine], 1), jnp.concatenate([-sine, sine], 1)


VMEM = pl.BlockSpec(memory_space=pltpu.VMEM)
SMEM = pl.BlockSpec(memory_space=pltpu.SMEM)
ANY = pl.BlockSpec(memory_space=pl.ANY)
HBM = pl.BlockSpec(memory_space=pltpu.HBM)


def params(mib):
    return pltpu.CompilerParams(vmem_limit_bytes=mib * 2**20)


def stage_body(n, flag, *refs):
    own, other, outs, sems = refs[:n], refs[n : 2 * n], refs[-5:-1], refs[-1]

    def bring(first, second):
        copies = []
        for half, sources in enumerate((first, second)):
            q_out, kv_out = outs[2 * half], outs[2 * half + 1]
            nk = sources[1].shape[1]
            targets = (q_out, kv_out.at[:, pl.ds(0, nk)], kv_out.at[:, pl.ds(nk, nk)])
            for i, (source, target) in enumerate(zip(sources, targets)):
                copies.append(pltpu.make_async_copy(source, target, sems.at[half, i]))
        for copy in copies:
            copy.start()
        for copy in copies:
            copy.wait()

    @pl.when(flag[0] == 1)
    def _():
        bring(own, other)

    @pl.when(flag[0] != 1)
    def _():
        bring(other, own)


def stage(flag, own, other, deps):
    half, nq = own[0].shape
    nk = own[1].shape[1]
    shapes = [pltpu.VMEM((half, nq), jnp.bfloat16), pltpu.VMEM((half, 2 * nk), jnp.bfloat16)] * 2
    return pl.pallas_call(
        functools.partial(stage_body, len(own)),
        out_shape=tuple(shapes),
        in_specs=[SMEM] + [HBM] * (2 * len(own)) + [ANY] * len(deps),
        out_specs=(VMEM,) * 4,
        scratch_shapes=[pltpu.SemaphoreType.DMA((2, len(own)))],
        compiler_params=params(2),
        cost_estimate=pl.CostEstimate(flops=0, bytes_accessed=4 * half * (nq + 2 * nk), transcendentals=0),
        name="stage",
    )(flag, *own, *other, *deps)


def project_body(row, tile, rot, keep, ta, tb, wa, wb, bias, cos, sin, *refs):
    out = refs[-2] if keep else refs[-1]
    if keep:
        refs[-1][...] = tb[...]
    rows = tb.shape[0]
    mine = pl.ds(row, rows)

    def columns(i):
        at = pl.ds(pl.multiple_of(i * tile, tile), tile)
        acc = jnp.dot(ta[mine, :], wa[:, at], preferred_element_type=jnp.float32)
        acc = acc + jnp.dot(tb[...], wb[:, at], preferred_element_type=jnp.float32)
        acc = acc + bias[:, at]
        heads = []
        for h in range(tile // HD):
            v = acc[:, h * HD : (h + 1) * HD]
            if h < rot:
                v = v * cos[mine, :] + pltpu.roll(v, HD // 2, 1) * sin[mine, :]
            heads.append(v.astype(jnp.bfloat16))
        out[:, at] = jnp.concatenate(heads, 1)

    if tile == out.shape[1]:
        columns(0)
    else:
        pl.loop(0, out.shape[1] // tile)(columns)


def project(tokens, row, piece, wa, wb, bias, cos, sin, tile, rot, deps, keep=False):
    rows, half = piece.shape
    cols = wa.shape[1]
    out = jax.ShapeDtypeStruct((rows, cols), jnp.bfloat16)
    return pl.pallas_call(
        functools.partial(project_body, row, tile, rot, keep),
        out_shape=(out, pltpu.VMEM(piece.shape, piece.dtype)) if keep else out,
        in_specs=[VMEM] * 7 + [ANY] * len(deps),
        out_specs=(VMEM, VMEM) if keep else VMEM,
        compiler_params=params(5),
        cost_estimate=pl.CostEstimate(flops=4 * rows * half * cols, bytes_accessed=0, transcendentals=0),
    )(tokens, piece, wa, wb, bias, cos, sin, *deps)


def attend_body(plan, n_arrays, q_row, groups, per, v_base, n_sent, bias, query, *refs):
    arrays = refs[:n_arrays]
    held = refs[-1]
    outs = refs[n_arrays:-1][-2:] if n_sent < groups * per else refs[-2:-1]
    scale = math.log2(math.e) / math.sqrt(HD)
    lower = lax.broadcasted_iota(jnp.int32, (BLOCK, BLOCK), 0) >= lax.broadcasted_iota(
        jnp.int32, (BLOCK, BLOCK), 1
    )
    rows = lambda r: slice(r * BLOCK, (r + 1) * BLOCK)

    def kv_head(g):
        for j, slots in enumerate(plan):
            n = len(slots)
            k_at = pl.ds(pl.multiple_of(g * HD, HD), HD)
            v_at = pl.ds(pl.multiple_of(v_base + g * HD, HD), HD)
            keys = jnp.concatenate([arrays[a][rows(r), k_at] for a, r in slots], 0)
            vals = jnp.concatenate([arrays[a][rows(r), v_at] for a, r in slots], 0)
            vals = jnp.concatenate([vals, jnp.ones_like(vals)], 1)
            for h in range(per):
                at = pl.ds(pl.multiple_of((g * per + h) * HD, HD), HD)
                s = lax.dot_general(
                    query[rows(q_row + j), at], keys, (((1,), (1,)), ((), ())),
                    preferred_element_type=jnp.float32,
                )
                parts = [jnp.where(lower, s[:, :BLOCK], -1e30)]
                for t in range(1, n):
                    parts.append(s[:, t * BLOCK : (t + 1) * BLOCK] + bias[j * n + t])
                s = jnp.concatenate(parts, 1)
                peak = jnp.max(s, axis=1, keepdims=True)
                p = jnp.exp2((s - peak) * scale).astype(jnp.bfloat16)
                o = jnp.dot(p, vals, preferred_element_type=jnp.float32)
                held[rows(j), at] = (o[:, :HD] / o[:, HD:]).astype(jnp.bfloat16)

    if groups == 1:
        kv_head(0)
    else:
        pl.loop(0, groups)(kv_head)
    outs[0][...] = held[:, : n_sent * HD]
    if len(outs) > 1:
        outs[1][...] = held[:, n_sent * HD :]


def attend(bias, query, q_row, arrays, plan, groups, per, v_base, n_sent, deps):
    nb = len(plan)
    heads = groups * per
    keys = len(plan[0]) * BLOCK
    shapes = [jax.ShapeDtypeStruct((nb * BLOCK, n * HD), jnp.bfloat16) for n in (n_sent, heads - n_sent) if n]
    return pl.pallas_call(
        functools.partial(attend_body, plan, len(arrays), q_row, groups, per, v_base, n_sent),
        out_shape=tuple(shapes),
        in_specs=[SMEM] + [VMEM] * (1 + len(arrays)) + [ANY] * len(deps),
        out_specs=(VMEM,) * len(shapes),
        scratch_shapes=[pltpu.VMEM((nb * BLOCK, heads * HD), jnp.bfloat16)],
        compiler_params=params(5),
        cost_estimate=pl.CostEstimate(
            flops=4 * nb * heads * HD * keys * BLOCK,
            bytes_accessed=0,
            transcendentals=nb * BLOCK * heads * keys,
        ),
        name="attend",
    )(bias, query, *arrays, *deps)


def order_body(flag, own, other, first, second, sems):
    def bring(sources):
        copies = [
            pltpu.make_async_copy(source, target, sems.at[i])
            for i, (source, target) in enumerate(zip(sources, (first, second)))
        ]
        for copy in copies:
            copy.start()
        for copy in copies:
            copy.wait()

    @pl.when(flag[0] == 1)
    def _():
        bring((own, other))

    @pl.when(flag[0] != 1)
    def _():
        bring((other, own))


def order_halves(flag, own, other, deps):
    half = pltpu.VMEM(own.shape, own.dtype)
    return pl.pallas_call(
        lambda *refs: order_body(*refs[:3], *refs[-3:]),
        out_shape=(half, half),
        in_specs=[SMEM] + [HBM] * 2 + [ANY] * len(deps),
        out_specs=(VMEM, VMEM),
        scratch_shapes=[pltpu.SemaphoreType.DMA((2,))],
        compiler_params=params(2),
        cost_estimate=pl.CostEstimate(flops=0, bytes_accessed=4 * own.size, transcendentals=0),
        name="order_halves",
    )(flag, own, other, *deps)


def project_shared_body(bases, ta, *refs):
    n_pieces = len(bases)
    pieces = refs[:n_pieces]
    wa, wb, bias, cos, sin = refs[n_pieces : n_pieces + 5]
    out, kv_out = refs[-2:]
    rows = pieces[0].shape[0]
    for i, tb in enumerate(pieces):
        mine = slice(bases[i], bases[i] + rows)
        here = slice(i * rows, (i + 1) * rows)

        def columns(t, last):
            at = pl.ds(pl.multiple_of(t * 2 * HD, 2 * HD), 2 * HD)
            acc = jnp.dot(ta[mine, :], wa[:, at], preferred_element_type=jnp.float32)
            acc = acc + jnp.dot(tb[...], wb[:, at], preferred_element_type=jnp.float32)
            acc = acc + bias[:, at]
            heads = []
            for h in range(2):
                v = acc[:, h * HD : (h + 1) * HD]
                if not (last and h):
                    v = v * cos[mine, :] + pltpu.roll(v, HD // 2, 1) * sin[mine, :]
                heads.append(v.astype(jnp.bfloat16))
            return jnp.concatenate(heads, 1)

        for t in range(SHARED // 2):
            out[here, t * 2 * HD : (t + 1) * 2 * HD] = columns(t, False)
        kv_out[here, :] = columns(SHARED // 2, True)


def project_shared(tokens, bases, pieces, wa, wb, bias, cos, sin, deps):
    rows, half = pieces[0].shape
    total = rows * len(pieces)
    cols = wa.shape[1]
    return pl.pallas_call(
        functools.partial(project_shared_body, bases),
        out_shape=(
            jax.ShapeDtypeStruct((total, SHARED * HD), jnp.bfloat16),
            jax.ShapeDtypeStruct((total, 2 * HD), jnp.bfloat16),
        ),
        in_specs=[VMEM] * (len(pieces) + 6) + [ANY] * len(deps),
        out_specs=(VMEM, VMEM),
        compiler_params=params(5),
        cost_estimate=pl.CostEstimate(flops=4 * total * half * cols, bytes_accessed=0, transcendentals=0),
        name="project_shared",
    )(tokens, *pieces, wa, wb, bias, cos, sin, *deps)


def cut_weights_body(index, wq, wk, wv, out, sems):
    n = out.shape[0]
    rows = pl.ds(pl.multiple_of(index[0] * n, 16), n)
    width = SHARED * HD
    copies = [
        pltpu.make_async_copy(
            wq.at[rows, pl.ds(wq.shape[1] - width, width)], out.at[:, pl.ds(0, width)], sems.at[0]
        ),
        pltpu.make_async_copy(
            wk.at[rows, pl.ds(wk.shape[1] - HD, HD)], out.at[:, pl.ds(width, HD)], sems.at[1]
        ),
        pltpu.make_async_copy(
            wv.at[rows, pl.ds(wv.shape[1] - HD, HD)], out.at[:, pl.ds(width + HD, HD)], sems.at[2]
        ),
    ]
    for copy in copies:
        copy.start()
    for copy in copies:
        copy.wait()


def cut_weights(index, weights, parts):
    n = weights[0].shape[0] // parts
    cols = (SHARED + 2) * HD
    return pl.pallas_call(
        cut_weights_body,
        out_shape=pltpu.VMEM((n, cols), jnp.bfloat16),
        in_specs=[SMEM] + [HBM] * 3,
        out_specs=VMEM,
        scratch_shapes=[pltpu.SemaphoreType.DMA((3,))],
        compiler_params=params(2),
        cost_estimate=pl.CostEstimate(flops=0, bytes_accessed=4 * n * cols, transcendentals=0),
        name="cut_weights",
    )(index, *weights)


def gather_body(n, order, *refs):
    pieces, out, sems = refs[:n], refs[-2], refs[-1]
    rows = pieces[0].shape[0]
    copies = []
    for i, piece in enumerate(pieces):
        at = pl.ds(pl.multiple_of(order[i] * rows, 16), rows)
        copies.append(pltpu.make_async_copy(piece, out.at[at, :], sems.at[i]))
    for copy in copies:
        copy.start()
    for copy in copies:
        copy.wait()


def gather(order, pieces, deps):
    rows, cols = pieces[0].shape
    return pl.pallas_call(
        functools.partial(gather_body, len(pieces)),
        out_shape=pltpu.VMEM((rows * len(pieces), cols), jnp.bfloat16),
        in_specs=[SMEM] + [ANY] * (len(pieces) + len(deps)),
        out_specs=VMEM,
        scratch_shapes=[pltpu.SemaphoreType.DMA((len(pieces),))],
        compiler_params=params(6),
        cost_estimate=pl.CostEstimate(
            flops=0, bytes_accessed=4 * rows * cols * len(pieces), transcendentals=0
        ),
        name="gather",
    )(order, *pieces, *deps)


def cut_body(row, source, out, sem):
    copy = pltpu.make_async_copy(source.at[pl.ds(row, out.shape[0]), :], out, sem)
    copy.start()
    copy.wait()


def cut(source, block, count):
    return pl.pallas_call(
        functools.partial(cut_body, block * BLOCK),
        out_shape=pltpu.VMEM((count * BLOCK, source.shape[1]), source.dtype),
        in_specs=[HBM],
        out_specs=VMEM,
        scratch_shapes=[pltpu.SemaphoreType.DMA],
        compiler_params=params(2),
        cost_estimate=pl.CostEstimate(
            flops=0, bytes_accessed=2 * count * BLOCK * source.shape[1], transcendentals=0
        ),
        name="cut",
    )(source)


def place_body(items, sides, *refs):
    out, sems = refs[-2:]
    copies = []
    for i, (first, side) in enumerate(items):
        rows, cols = refs[i].shape
        at = pl.ds(pl.multiple_of(sides[side] * HD, HD), cols)
        copies.append(
            pltpu.make_async_copy(refs[i], out.at[pl.ds(first * BLOCK, rows), at], sems.at[i])
        )
    for copy in copies:
        copy.start()
    for copy in copies:
        copy.wait()


def place(total, sides, items, shape, deps=()):
    arrays = [array for array, _, _ in items]
    rest = list(deps) if total is None else [*deps, total]
    aliases = {} if total is None else {len(arrays) + len(rest): 0}
    return pl.pallas_call(
        functools.partial(place_body, [(first, side) for _, first, side in items]),
        out_shape=jax.ShapeDtypeStruct(shape, jnp.bfloat16),
        in_specs=[SMEM] + [VMEM] * len(arrays) + [ANY] * len(deps) + ([] if total is None else [HBM]),
        out_specs=HBM,
        scratch_shapes=[pltpu.SemaphoreType.DMA((len(arrays),))],
        input_output_aliases=aliases,
        compiler_params=params(3),
        cost_estimate=pl.CostEstimate(
            flops=0, bytes_accessed=4 * sum(a.size for a in arrays), transcendentals=0
        ),
        name="place",
    )(sides, *arrays, *rest)


def chunks_of(blocks):
    n = blocks // 4
    return [(quarter * n, n) for quarter in (2, 0, 1, 3)]


def layer(tokens, q_weight, k_weight, v_weight, q_bias, v_bias):
    n_sub = lax.axis_size("sub")
    n_ctx = lax.axis_size("ctx")
    n_head = lax.axis_size("head")
    n_groups = lax.axis_size("groups")
    rows = tokens.shape[0]
    blocks = rows // BLOCK
    nq = q_weight.shape[1]
    kvl = k_weight.shape[1] // HD
    sub = lax.axis_index("sub")
    ctx = lax.axis_index("ctx")
    head = lax.axis_index("head")
    group = lax.axis_index("groups")
    shard = ctx * n_sub + sub
    runs = chunks_of(blocks)
    weights = (q_weight, k_weight, v_weight)

    paired = n_head == 2 and kvl == 2 and n_groups == 2
    if paired:
        parts = n_groups * n_ctx
        mine = (ctx * n_groups + group).astype(jnp.int32).reshape(1)
        part = cut_weights(mine, weights, parts)
        ring = [swapped(part, "head")]
        pieces = []
        for b, n in runs:
            pieces.append(swapped(cut(tokens, b, n), "head"))
        flag = (sub == head).astype(jnp.int32).reshape(1)
        shared_bias = jnp.concatenate(
            [q_bias[nq - SHARED * HD :], jnp.zeros((HD,), jnp.float32), v_bias[(kvl - 1) * HD :]]
        )[None, :]
        shared_bias = swapped(shared_bias, "head")
        for _ in range(1, n_ctx):
            ring.append(shifted(ring[-1], "ctx", 1))
        across = []
        for d in range(n_ctx):
            across.append(swapped(ring[d], "groups"))
        turn = jnp.arange(2 * n_ctx, dtype=jnp.int32)
        there = lax.rem(ctx + n_ctx - turn % n_ctx, n_ctx) * n_groups
        part_order = jnp.where(turn < n_ctx, there + group, there + 1 - group).astype(jnp.int32)
    else:
        features = lax.all_gather(tokens, "head", axis=1, tiled=True)
        half = features.shape[1] // n_sub
        flag = (sub == 0).astype(jnp.int32).reshape(1)
        tokens = features[:, :half]
        pieces = [features[b * BLOCK : (b + n) * BLOCK, half:] for b, n in runs]
    other = swapped(k_weight, "sub"), swapped(v_weight, "sub")
    other = (swapped(q_weight, "sub"),) + other
    qb = q_bias[None, :]
    kvb = jnp.concatenate([jnp.zeros_like(v_bias), v_bias])[None, :]
    positions = (shard * rows + jnp.arange(rows, dtype=jnp.int32)).astype(jnp.float32)
    cos, sin = rotary_tables(positions)

    far_steps = [s for s in (1, 2, 4, 8) if s < n_ctx]
    biases = []
    for b, n in runs:
        steps = jnp.array(list(NEAR) + [blocks] + [n_sub * blocks * s for s in far_steps], jnp.int32)
        places = shard * blocks + b + jnp.arange(n, dtype=jnp.int32)
        biases.append(jnp.where(places[:, None] >= steps[None, :], 0.0, -1e30).astype(jnp.float32).reshape(-1))
    small = [qb, kvb, cos, sin, *biases]
    if paired:
        columns = kvl * GROUP
        sides = columns * jnp.array([0, 1, 1, 2], jnp.int32) - SHARED * jnp.array([0, 1, 0, 1], jnp.int32)
        sides = sides + head.astype(jnp.int32) * columns * jnp.array([1, 1, -1, -1], jnp.int32)
        small += [sides, part_order]
    wqa, wkva, wqb, wkvb = stage(flag, weights, other, small)
    queries, sources = {}, {}
    shared_queries, shared_sources = {}, {}

    def exchanged(kv, places, table):
        held = {"own": kv}
        held["prev"] = shifted(kv, ("ctx", "sub"), 1)
        for s in far_steps:
            held["far", s] = shifted(kv, "ctx", 1) if s == 1 else shifted(held["far", s // 2], "ctx", s // 2)
        for r, b in enumerate(places):
            for name, array in held.items():
                table[name, b] = (array, r)

    def keys_values(i, deps):
        (b, n), piece = runs[i], pieces[i]
        kv = project(
            tokens, b * BLOCK, piece, wkva, wkvb, kvb, cos, sin, 2 * kvl * HD, kvl, deps,
            paired and i % 2 == 0,
        )
        if paired and i % 2 == 0:
            kv, pieces[i] = kv
        exchanged(kv, range(b, b + n), sources)
        return (kv,)

    def all_queries(i, deps):
        (b, n), piece = runs[i], pieces[i]
        tile = 2 * HD if nq % (2 * HD) == 0 else HD
        q = project(tokens, b * BLOCK, piece, wqa, wqb, qb, cos, sin, tile, tile // HD, deps)
        for r in range(n):
            queries[b + r] = (q, r)
        return (q,)

    def neighbours_head(which, deps):
        bases = [runs[i][0] * BLOCK for i in which]
        qkv, kv = project_shared(
            tokens, bases, [pieces[i] for i in which], *shared_weights, shared_bias, cos, sin, deps
        )
        exchanged(kv, [b for i in which for b in range(runs[i][0], sum(runs[i]))], shared_sources)
        r = 0
        for i in which:
            for b in range(runs[i][0], sum(runs[i])):
                shared_queries[b] = (qkv, r)
                r += 1
        return (kv,)

    def attention(i, kind, deps):
        b0, count = runs[i]
        pair = tuple(range(b0, b0 + count))
        if kind == "neighbour":
            qs, table, form = shared_queries, shared_sources, (1, SHARED, HD, SHARED)
        else:
            n_sent = kvl * GROUP - (SHARED if paired else 0)
            qs, table, form = queries, sources, (kvl, GROUP, kvl * HD, n_sent)
        arrays, plan = [], []
        for b in pair:
            slots = []
            wanted = [(d, ("own", b - d) if d <= b else ("prev", blocks + b - d)) for d in NEAR + (blocks,)]
            wanted += [(n_sub * blocks * s, (("far", s), b)) for s in far_steps]
            for d, key in wanted:
                array, r = table[key]
                at = next((k for k, a in enumerate(arrays) if a is array), None)
                if at is None:
                    at = len(arrays)
                    arrays.append(array)
                slots.append((at, r))
            plan.append(tuple(slots))
        return attend(biases[i], *qs[b0], arrays, plan, *form, deps)

    shape = (rows, n_head * nq)
    if not paired:
        deps = ()
        for i in range(len(runs)):
            deps = keys_values(i, deps)
            deps = all_queries(i, deps)
        outs = {}
        for i, (b, _) in enumerate(runs):
            outs[b] = attention(i, "own", deps)[0]
        local = jnp.concatenate([outs[b] for b in sorted(outs)], 0)
        return lax.all_gather(local, "head", axis=1, tiled=True)

    sent, received, kept, extra = {}, {}, {}, {}

    def send(i, deps):
        sent[i], kept[i] = attention(i, "own", deps)
        received[i] = swapped(sent[i], "head")
        return (kept[i],)

    def add(i, deps):
        extra[i] = attention(i, "neighbour", deps)[0]
        return (extra[i],)

    deps = (wqa,)
    deps = keys_values(0, deps)
    deps = all_queries(0, deps)
    deps = keys_values(1, deps)
    deps = all_queries(1, deps)
    gathered = gather(part_order, ring + across, deps)
    shared_other = swapped(gathered, "sub")
    shared_weights = order_halves(flag, gathered, shared_other, (gathered,))
    deps = neighbours_head((0, 1), (shared_weights[0],))
    deps = keys_values(2, deps)
    deps = send(0, deps)
    deps = all_queries(2, deps)
    deps = keys_values(3, deps)
    deps = neighbours_head((2, 3), deps)
    deps = send(1, deps)
    deps = send(2, deps)
    deps = all_queries(3, deps)
    deps = send(3, deps)
    deps = add(0, deps)
    deps = add(1, deps)
    first = lambda i: runs[i][0]
    total = place(
        None, sides,
        [(sent[i], first(i), 0) for i in range(4)] + [(kept[i], first(i), 1) for i in range(4)]
        + [(extra[i], first(i), 3) for i in (0, 1)],
        shape, deps,
    )
    deps = add(2, deps)
    deps = add(3, deps)
    total = place(
        total, sides,
        [(extra[i], first(i), 3) for i in (2, 3)] + [(received[i], first(i), 2) for i in (0, 1, 2)], shape,
    )
    return place(total, sides, [(received[3], first(3), 2)], shape)


def solution(mesh):
    return jax.shard_map(
        layer,
        mesh=mesh,
        in_specs=(
            P(("groups", "ctx", "sub"), "head"),
            P("sub", "head"),
            P("sub", "head"),
            P("sub", "head"),
            P("head"),
            P("head"),
        ),
        out_specs=P(("groups", "ctx", "sub"), None),
        check_vma=False,
    )
```
